32 devices in a mesh: ctx: 4 (over z), ch: 8 (over y, x, core).
Axes of the slice: x: 2, y: 2, z: 4, core: 2. Of those that a mesh axis runs over, the one named last changes fastest.
Arguments:
- inputs: bfloat16 [16384, 8192], P('ctx', 'ch'), may hold values from -6 to 6
- grad_output: bfloat16 [16384, 8192], P('ctx', 'ch'), may hold values from -6 to 6
- log_rate: float32 [16, 16], replicated
- rotation: float32 [16, 16], replicated, may hold values from -3.140625 to 3.140625
- res_re: float32 [16, 16], replicated, may hold values from -1.5 to 1.5
- res_im: float32 [16, 16], replicated, may hold values from -1.5 to 1.5
- skip_gain: float32 [8192], P('ch'), may hold values from -4 to 4
Outputs:
- grad_input: bfloat16 [16384, 8192], P('ctx', 'ch')
- grad_log_rate: float32 [16, 16], replicated
- grad_rotation: float32 [16, 16], replicated
- grad_res_re: float32 [16, 16], replicated
- grad_res_im: float32 [16, 16], replicated
- grad_skip: float32 [8192], P('ch')
The draws below stay inside these ranges and needn't reach their ends.
All inputs are finite; a program needn't handle non-finite values.
Results may differ from the reference program's by a relative error of at most 0.0055.
Values sent between devices are 32-bit elements; how exact they have to be, the bound alone decides.
No kernel may reach another device: no remote copies, remote signals or barrier semaphores. Data moves between devices by JAX's collectives and lax.ppermute only.
A program may use at most 192 MiB of HBM per device.

```python
import jax
import jax.numpy as jnp
from jax import lax

D = 8192
M = 16
GROUP_W = 512
BLOCK = 64
TOKENS = 16384
GROUPS = 16


def draw_log_rate(key, part):
    first_key, second_key, third_key = jax.random.split(jax.random.fold_in(key, 7), 3)
    slow_share = 0.5
    slow_mask = jax.random.bernoulli(first_key, slow_share, (M, GROUPS))
    slow_value = jnp.log(2.302585 / TOKENS) + jax.random.uniform(second_key, (M, GROUPS), jnp.float32, jnp.log(0.05), 0.0)
    fast_value = jax.random.uniform(third_key, (M, GROUPS), jnp.float32, jnp.log(1.0 / 50.0), jnp.log(1.0 / 30.0))
    return jnp.where(slow_mask, slow_value, fast_value).astype(jnp.float32)


def levels(key, extent, cuts, least, high):
    level = 1.0
    for position, shards_of in cuts:
        heights = jax.random.uniform(jax.random.fold_in(jax.random.fold_in(key, 6), position), (shards_of,), jnp.float32, least / len(cuts), high / len(cuts))
        level = level * jnp.repeat(jnp.exp(heights), extent[position] // shards_of).reshape((-1,) + (1,) * (len(extent) - 1 - position))
    return level


def centred(rng, extent, spread, reach, pieces=(), kind=jnp.bfloat16):
    level = levels(rng, extent, pieces, -0.22, 0.18) if pieces else 1.0
    entries = jax.random.normal(rng, extent, jnp.float32) * spread * level
    return jnp.minimum(jnp.maximum(entries, -reach), reach).astype(kind)


def setup_inputs(seed: int = 0) -> dict:
    key_list = jax.random.split(jax.random.key(seed), 8)
    return {
        "inputs": centred(key_list[0], (TOKENS, D), 1.0, 6.0, ((0, 4), (1, 8))),
        "grad_output": centred(key_list[1], (TOKENS, D), 1.0, 6.0, ((0, 4), (1, 8))),
        "log_rate": draw_log_rate(jax.random.fold_in(key_list[7], 71), 0),
        "rotation": jnp.clip(jax.random.uniform(key_list[3], (M, GROUPS), jnp.float32, -3.140625, 3.140625), -3.140625, 3.140625),
        "res_re": centred(key_list[4], (M, GROUPS), 0.25, 1.5, (), jnp.float32),
        "res_im": centred(key_list[5], (M, GROUPS), 0.25, 1.5, (), jnp.float32),
        "skip_gain": centred(key_list[6], (D,), 1.0, 4.0, ((0, 8),), jnp.float32),
    }


highest = lax.Precision.HIGHEST

def contract(form, left, right):
    return jnp.einsum(form, left, right, precision=highest)

def powers(decay_rate, rotation, steps):
    expanded = steps[..., None, None]
    magnitude = jnp.exp(-expanded * decay_rate)
    phases = expanded * rotation
    return (magnitude * jnp.cos(phases), magnitude * jnp.sin(phases))

def block_sums(x_blocks, dy_blocks, decay_rate, rotation):
    block_width = x_blocks.shape[1]
    offset = jnp.arange(block_width, dtype=jnp.float32)
    backward = block_width - 1.0 - offset
    back_re, back_im = powers(decay_rate, rotation, backward)
    lifted = backward[:, None, None]
    table_x = jnp.stack([back_re, back_im, lifted * back_re, lifted * back_im], 1)
    ahead_re, ahead_im = powers(decay_rate, rotation, offset)
    weight = (offset + 1.0)[:, None, None]
    table_y = jnp.stack([ahead_re, -ahead_im, weight * ahead_re, -weight * ahead_im], 1)
    x_sums = contract('btgc,tkmg->bkmgc', x_blocks.astype(jnp.float32), table_x)
    y_sums = contract('btgc,tkmg->bkmgc', dy_blocks.astype(jnp.float32), table_y)
    return (x_sums, y_sums)

def block_chain(x_sums, y_sums, decay_rate, rotation, mode_gain, block_width):
    block_count = x_sums.shape[0]
    block_index = jnp.arange(block_count, dtype=jnp.float32)
    block_lag = block_index[:, None] - block_index[None, :] - 1.0
    kernel_re, kernel_im = powers(decay_rate, rotation, jnp.maximum(block_lag, 0.0) * block_width)
    causal = (block_lag >= 0.0).astype(jnp.float32)[:, :, None, None]
    kernel_re = kernel_re * causal
    kernel_im = kernel_im * causal
    scaled = mode_gain[:, :, None]
    input_re = scaled * x_sums[:, 0]
    input_im = scaled * x_sums[:, 1]
    state_re = contract('abmg,bmgc->amgc', kernel_re, input_re) - contract('abmg,bmgc->amgc', kernel_im, input_im)
    state_im = contract('abmg,bmgc->amgc', kernel_re, input_im) + contract('abmg,bmgc->amgc', kernel_im, input_re)
    tail_re, tail_im = powers(decay_rate, rotation, (block_count - 1.0 - block_index) * block_width)
    end_re = lax.optimization_barrier(jnp.sum(tail_re[..., None] * input_re - tail_im[..., None] * input_im, 0))
    end_im = lax.optimization_barrier(jnp.sum(tail_re[..., None] * input_im + tail_im[..., None] * input_re, 0))
    drive_re = y_sums[:, 0]
    drive_im = y_sums[:, 1]
    after_re = contract('bamg,bmgc->amgc', kernel_re, drive_re) + contract('bamg,bmgc->amgc', kernel_im, drive_im)
    after_im = contract('bamg,bmgc->amgc', kernel_re, drive_im) - contract('bamg,bmgc->amgc', kernel_im, drive_re)
    head_re, head_im = powers(decay_rate, rotation, block_index * block_width)
    start_re = lax.optimization_barrier(jnp.sum(head_re[..., None] * drive_re + head_im[..., None] * drive_im, 0))
    start_im = lax.optimization_barrier(jnp.sum(head_re[..., None] * drive_im - head_im[..., None] * drive_re, 0))
    states = (state_re, state_im, after_re, after_im)
    return (states, (end_re, end_im, start_re, start_im), (head_re, head_im, tail_re, tail_im))

def finish(x_blocks, dy_blocks, x_sums, y_sums, states, correlation, decay_rate, rotation, mode_gain, res_re, res_im, skip_gain):
    block_width = x_blocks.shape[1]
    state_re, state_im, after_re, after_im = states
    step_re, step_im = powers(decay_rate, rotation, jnp.ones((), jnp.float32))
    step_re = step_re[:, :, None]
    step_im = step_im[:, :, None]
    full_re, full_im = powers(decay_rate, rotation, jnp.ones((), jnp.float32) * block_width)
    full_re = full_re[:, :, None]
    full_im = full_im[:, :, None]
    gain_col = mode_gain[:, :, None]
    drive_re = y_sums[:, 0]
    drive_im = y_sums[:, 1]
    turn_re = step_re * drive_re + step_im * drive_im
    turn_im = step_re * drive_im - step_im * drive_re
    first_re = lax.optimization_barrier(jnp.sum(state_re * turn_re + state_im * turn_im, (0, 3)))
    first_im = lax.optimization_barrier(jnp.sum(state_re * turn_im - state_im * turn_re, (0, 3)))
    meet_re = after_re * x_sums[:, 0] + after_im * x_sums[:, 1]
    meet_im = after_im * x_sums[:, 0] - after_re * x_sums[:, 1]
    third_re = lax.optimization_barrier(jnp.sum(step_re * meet_re + step_im * meet_im, (0, 3)))
    third_im = lax.optimization_barrier(jnp.sum(step_re * meet_im - step_im * meet_re, (0, 3)))
    cross_re = state_re * after_re + state_im * after_im
    cross_im = state_re * after_im - state_im * after_re
    second_re = lax.optimization_barrier(jnp.sum(block_width * (full_re * cross_re + full_im * cross_im) + state_re * y_sums[:, 2] + state_im * y_sums[:, 3] + gain_col * (after_re * x_sums[:, 2] + after_im * x_sums[:, 3]), (0, 3)))
    second_im = lax.optimization_barrier(jnp.sum(block_width * (full_re * cross_im - full_im * cross_re) + state_re * y_sums[:, 3] - state_im * y_sums[:, 2] + gain_col * (after_im * x_sums[:, 2] - after_re * x_sums[:, 3]), (0, 3)))
    offset = jnp.arange(block_width, dtype=jnp.float32)
    lag_map = (offset[None, :, None] - offset[None, None, :] == offset[:, None, None]).astype(jnp.float32)
    lagged = contract('nts,tsgc->ngc', lag_map, correlation)
    weight_sum = lax.optimization_barrier(jnp.sum(lagged, 2))[:, None, :]
    near_re, near_im = powers(decay_rate, rotation, offset)
    intra_re = lax.optimization_barrier(jnp.sum(near_re * weight_sum, 0))
    intra_im = -lax.optimization_barrier(jnp.sum(near_im * weight_sum, 0))
    prior_re, prior_im = powers(decay_rate, rotation, jnp.maximum(offset - 1.0, 0.0))
    ramp = offset[:, None, None]
    inner_re = lax.optimization_barrier(jnp.sum(ramp * prior_re * weight_sum, 0))
    inner_im = -lax.optimization_barrier(jnp.sum(ramp * prior_im * weight_sum, 0))
    partials = (first_re + mode_gain * intra_re, first_im + mode_gain * intra_im, second_re + mode_gain * inner_re, second_im + mode_gain * inner_im, third_re + intra_re, third_im + intra_im)
    spacing = offset[None, :] - offset[:, None]
    lift_re, lift_im = powers(decay_rate, rotation, jnp.maximum(spacing, 0.0))
    kernel_rows = lax.optimization_barrier(jnp.sum(mode_gain * (res_re * lift_re - res_im * lift_im), 2))
    kernel_rows = kernel_rows * (spacing >= 0.0).astype(jnp.float32)[:, :, None]
    dy_float = dy_blocks.astype(jnp.float32)
    near = contract('tsg,bsgc->btgc', kernel_rows, dy_float)
    far_re, far_im = powers(decay_rate, rotation, block_width - offset)
    pull_re = mode_gain * (res_re * far_re - res_im * far_im)
    pull_im = mode_gain * (res_re * far_im + res_im * far_re)
    far = contract('tmg,bmgc->btgc', pull_re, after_re) + contract('tmg,bmgc->btgc', pull_im, after_im)
    result = near + far + skip_gain[None, None] * dy_float
    return (result, partials, lagged[0])

def to_grads(partials, decay_rate, rotation, mode_gain, res_re, res_im):
    first_re, first_im, second_re, second_im, third_re, third_im = partials
    step_re, step_im = powers(decay_rate, rotation, jnp.ones((), jnp.float32))
    twist_re = res_re * second_re + res_im * second_im
    twist_im = res_re * second_im - res_im * second_re
    gain_term = res_re * third_re + res_im * third_im
    pull_re = twist_re * step_re + twist_im * step_im
    pull_im = twist_re * step_im - twist_im * step_re
    slope = jnp.exp(-2.0 * decay_rate) / mode_gain
    grad_rate = decay_rate * (slope * gain_term - pull_re)
    return jnp.stack([grad_rate, -pull_im, first_re, first_im])

def reference(inputs, grad_output, log_rate, rotation, res_re, res_im, skip_gain):
    groups = D // GROUP_W

    def one_group(packed):
        x_group, dy_group, rate_col, angle_col, real_col, imag_col, skip_col = packed
        x_blocks = x_group.reshape(TOKENS // BLOCK, BLOCK, 1, GROUP_W)
        dy_blocks = dy_group.reshape(TOKENS // BLOCK, BLOCK, 1, GROUP_W)
        decay_rate = jnp.exp(rate_col)[:, None]
        angle_here = angle_col[:, None]
        real_here = real_col[:, None]
        imag_here = imag_col[:, None]
        mode_gain = jnp.sqrt(-jnp.expm1(-2.0 * decay_rate))
        x_sums, y_sums = block_sums(x_blocks, dy_blocks, decay_rate, angle_here)
        states, summaries, tables = block_chain(x_sums, y_sums, decay_rate, angle_here, mode_gain, BLOCK)
        correlation = contract('btgc,bsgc->tsgc', dy_blocks.astype(jnp.float32), x_blocks.astype(jnp.float32))
        result, partials, skip_grads = finish(x_blocks, dy_blocks, x_sums, y_sums, states, correlation, decay_rate, angle_here, mode_gain, real_here, imag_here, skip_col[None, :])
        grads = to_grads(partials, decay_rate, angle_here, mode_gain, real_here, imag_here)
        return (result.reshape(TOKENS, GROUP_W).astype(jnp.bfloat16), grads[:, :, 0], skip_grads[0])
    packed = (inputs.reshape(TOKENS, groups, GROUP_W).transpose(1, 0, 2), grad_output.reshape(TOKENS, groups, GROUP_W).transpose(1, 0, 2), log_rate.T, rotation.T, res_re.T, res_im.T, skip_gain.reshape(groups, GROUP_W))
    dx_all, grads_all, skip_all = lax.map(one_group, packed)
    grad_input = dx_all.transpose(1, 0, 2).reshape(TOKENS, D)
    grads = grads_all.transpose(1, 2, 0)
    return (grad_input, grads[0], grads[1], grads[2], grads[3], skip_all.reshape(D))
```

```python
import functools

import jax
import jax.numpy as jnp
from jax import lax
from jax.experimental import pallas as pl
from jax.experimental.pallas import tpu as pltpu
from jax.sharding import PartitionSpec as P

GROUP_W = 512
L = 256
CHUNK = 512

f32 = jnp.float32
bf16 = jnp.bfloat16
LANES = 128


def dot(a, b):
    return jnp.dot(a, b, preferred_element_type=f32)


def group_column(ref, group):
    table = ref[...]
    lane = lax.broadcasted_iota(jnp.int32, table.shape, 1)
    return jnp.sum(jnp.where(lane == group, table, 0.0), axis=1, keepdims=True)


def powers(rate, angle, steps):
    magnitude = jnp.exp(-steps * rate)
    phase = steps * angle
    return magnitude * jnp.cos(phase), magnitude * jnp.sin(phase)


def cmul(a, b):
    return a[0] * b[0] - a[1] * b[1], a[0] * b[1] + a[1] * b[0]


def conj(a):
    return a[0], -a[1]


def cdot(a, b):
    return a[0] * b[0] + a[1] * b[1], a[0] * b[1] - a[1] * b[0]


def add(a, b):
    return a[0] + b[0], a[1] + b[1]


def scale(s, a):
    return s * a[0], s * a[1]


def split(parts):
    lead = [p.astype(bf16) for p in parts]
    rest = [(p - h.astype(f32)).astype(bf16) for p, h in zip(parts, lead)]
    return jnp.concatenate(lead + rest, axis=0)


def positions(modes):
    return lax.broadcasted_iota(jnp.int32, (modes, L), 1).astype(f32)


def first_group(width):
    return lax.axis_index("ch") * width // GROUP_W


def lane_sum(a):
    return jnp.sum(a, axis=1, keepdims=True)


def sums_kernel(n, x_hbm, dy_hbm, lr_ref, ro_ref, *refs):
    sends = refs[: n - 1]
    e_ref, y_ref, skip_ref, x_buf, dy_buf, tx, ty, sem = refs[n - 1 :]
    steps, width = x_hbm.shape
    modes = lr_ref.shape[0]
    share = min(width, GROUP_W)
    groups = width // share
    chunks = steps // CHUNK
    blocks = steps // L
    copies = []
    for c in range(chunks):
        rows = pl.ds(c * CHUNK, CHUNK)
        pair = (
            pltpu.make_async_copy(x_hbm.at[rows], x_buf.at[rows], sem.at[0, c]),
            pltpu.make_async_copy(dy_hbm.at[rows], dy_buf.at[rows], sem.at[1, c]),
        )
        for copy in pair:
            copy.start()
        copies.append(pair)
    base = first_group(width)
    offset = positions(modes)
    for g in range(groups):
        rate = jnp.exp(group_column(lr_ref, base + g))
        angle = group_column(ro_ref, base + g)
        leap = powers(rate, angle, float(L))
        back = powers(rate, angle, (L - 1.0) - offset)
        ahead = conj(powers(rate, angle, offset))
        for b in range(blocks):
            tx[g, :, pl.ds((blocks - 1 - b) * L, L)] = split(back)
            ty[g, :, pl.ds(b * L, L)] = split(ahead)
            back = cmul(back, leap)
            ahead = cmul(ahead, conj(leap))
    direct = jnp.zeros((8, width), f32)
    for c in range(chunks):
        rows = slice(c * CHUNK, (c + 1) * CHUNK)
        for copy in copies[c]:
            copy.wait()
        for g in range(groups):
            cols = slice(g * share, (g + 1) * share)
            fwd = dot(tx[g, :, rows], x_buf[rows, cols])
            bwd = dot(ty[g, :, rows], dy_buf[rows, cols])
            fwd = fwd[: 2 * modes] + fwd[2 * modes :]
            bwd = bwd[: 2 * modes] + bwd[2 * modes :]
            if c == 0:
                e_ref[:, cols] = fwd
                y_ref[:, cols] = bwd
            else:
                e_ref[:, cols] += fwd
                y_ref[:, cols] += bwd
        prod = x_buf[rows, :].astype(f32) * dy_buf[rows, :].astype(f32)
        direct = direct + jnp.sum(prod.reshape(CHUNK // 8, 8, width), axis=0)
    total = jnp.sum(direct, axis=0, keepdims=True)
    me = lax.axis_index("ctx")
    e_all = e_ref[...]
    y_all = y_ref[...]
    tiles = width // LANES
    for t in range(tiles):
        skip_ref[t : t + 1, :] = total[:, t * LANES : (t + 1) * LANES]
    if tiles < 8:
        skip_ref[tiles:8, :] = jnp.zeros((8 - tiles, LANES), f32)
    for s in range(1, n):
        out = sends[s - 1]
        forward = me + s < n
        chosen = jnp.where(forward, e_all, y_all)
        for t in range(tiles):
            out[t * 2 * modes : (t + 1) * 2 * modes, :] = chosen[:, t * LANES : (t + 1) * LANES]
        out[tiles * 2 * modes :, :] = skip_ref[...]


def shard_sums(n, x, dy, log_rate, rotation):
    steps, width = x.shape
    modes = log_rate.shape[0]
    groups = max(1, width // GROUP_W)
    chunks = steps // CHUNK
    tiles = width // LANES
    extra = max(8, tiles)
    packed = jax.ShapeDtypeStruct((tiles * 2 * modes + extra, LANES), f32)
    state = jax.ShapeDtypeStruct((2 * modes, width), f32)
    vmem = pl.BlockSpec(memory_space=pltpu.VMEM)
    hbm = pl.BlockSpec(memory_space=pl.ANY)
    return pl.pallas_call(
        functools.partial(sums_kernel, n),
        in_specs=[hbm, hbm, vmem, vmem],
        out_specs=[vmem] * (n + 2),
        out_shape=[packed] * (n - 1) + [state, state, jax.ShapeDtypeStruct((extra, LANES), f32)],
        scratch_shapes=[
            pltpu.VMEM((steps, width), bf16),
            pltpu.VMEM((steps, width), bf16),
            pltpu.VMEM((groups, 4 * modes, steps), bf16),
            pltpu.VMEM((groups, 4 * modes, steps), bf16),
            pltpu.SemaphoreType.DMA((2, chunks)),
        ],
        cost_estimate=pl.CostEstimate(
            flops=8 * modes * steps * width * 2, bytes_accessed=4 * steps * width, transcendentals=0
        ),
        name="shard_sums",
    )(x, dy, log_rate, rotation)


def inner_kernel(x_hbm, dy_hbm, lr_ref, ro_ref, out_ref, xp_ref, yp_ref, x_buf, dy_buf, tx, ty, corr, state, acc, sem):
    steps, width = x_hbm.shape
    modes = lr_ref.shape[0]
    share = min(width, GROUP_W)
    groups = width // share
    chunks = steps // CHUNK
    blocks = steps // L
    per = CHUNK // L
    copies = []
    for c in range(chunks):
        rows = pl.ds(c * CHUNK, CHUNK)
        pair = (
            pltpu.make_async_copy(x_hbm.at[rows], x_buf.at[rows], sem.at[0, c]),
            pltpu.make_async_copy(dy_hbm.at[rows], dy_buf.at[rows], sem.at[1, c]),
        )
        for copy in pair:
            copy.start()
        copies.append(pair)
    base = first_group(width)
    offset = positions(modes)
    coeffs = []
    for g in range(groups):
        rate = jnp.exp(group_column(lr_ref, base + g))
        angle = group_column(ro_ref, base + g)
        leap = powers(rate, angle, float(L))
        behind = (L - 1.0) - offset
        back = powers(rate, angle, behind)
        ahead = conj(powers(rate, angle, offset))
        tx[g] = split([*back, *scale(behind, back)])
        ty[g] = split([*ahead, *scale(offset + 1.0, ahead)])
        coeffs.append((rate, angle, leap, ahead))
    state[...] = jnp.zeros_like(state)
    acc[...] = jnp.zeros_like(acc)
    yp_ref[...] = jnp.zeros_like(yp_ref)
    corr[...] = jnp.zeros_like(corr)
    m2, m3, m4 = 2 * modes, 3 * modes, 4 * modes
    reach = [(jnp.ones_like(coeffs[0][0]), jnp.zeros_like(coeffs[0][0]))] * groups
    for c in range(chunks):
        for copy in copies[c]:
            copy.wait()
        for b in range(c * per, (c + 1) * per):
            rows = slice(b * L, (b + 1) * L)
            for g in range(groups):
                rate, angle, leap, ahead = coeffs[g]
                cols = slice(g * share, (g + 1) * share)
                xb = x_buf[rows, cols]
                yb = dy_buf[rows, cols]
                corr[g] += lax.dot_general(
                    xb, yb, (((1,), (1,)), ((), ())), preferred_element_type=f32
                )
                xs = dot(tx[g], xb)
                xs = xs[:m4] + xs[m4:]
                ys = dot(ty[g], yb)
                ys = ys[:m4] + ys[m4:]
                x0, x1 = (xs[:modes], xs[modes:m2]), (xs[m2:m3], xs[m3:])
                y0, y1 = (ys[:modes], ys[modes:m2]), (ys[m2:m3], ys[m3:])
                e = state[0:modes, cols], state[modes:m2, cols]
                ep = state[m2:m3, cols], state[m3:m4, cols]
                third = cdot(e, y0)
                second = add(cdot(ep, y0), cdot(e, y1))
                acc[0:modes, cols] += third[0]
                acc[modes:m2, cols] += third[1]
                acc[m2:m3, cols] += second[0]
                acc[m3:m4, cols] += second[1]
                ep = add(cmul(leap, add(ep, scale(float(L), e))), x1)
                e = add(cmul(leap, e), x0)
                state[0:modes, cols], state[modes:m2, cols] = e
                state[m2:m3, cols], state[m3:m4, cols] = ep
                far = add(y1, scale(float(b * L), y0))
                far = cmul(conj(reach[g]), far)
                yp_ref[0:modes, cols] += far[0]
                yp_ref[modes:m2, cols] += far[1]
                reach[g] = cmul(reach[g], leap)
    xp_ref[...] = state[m2:m4, :]
    row = lax.broadcasted_iota(jnp.int32, (L, L), 0)
    lane = lax.broadcasted_iota(jnp.int32, (L, L), 1)
    out_lane = lax.broadcasted_iota(jnp.int32, (modes, LANES), 1)
    out = jnp.zeros((modes, LANES), f32)
    for g in range(groups):
        rate, angle, leap, ahead = coeffs[g]
        cols = slice(g * share, (g + 1) * share)
        lagged = jnp.where(lane >= row, corr[g], 0.0)
        bit = 1
        while bit < L:
            lagged = jnp.where((row & bit) != 0, pltpu.roll(lagged, L - bit, 1), lagged)
            bit *= 2
        lags = jnp.sum(lagged, axis=0, keepdims=True)
        step = powers(rate, angle, 1.0)
        third = cmul(conj(step), (lane_sum(acc[0:modes, cols]), lane_sum(acc[modes:m2, cols])))
        second = lane_sum(acc[m2:m3, cols]), lane_sum(acc[m3:m4, cols])
        third = add(third, (lane_sum(ahead[0] * lags), lane_sum(ahead[1] * lags)))
        prior = conj(powers(rate, angle, jnp.maximum(offset - 1.0, 0.0)))
        ramp = offset * lags
        second = add(second, (lane_sum(prior[0] * ramp), lane_sum(prior[1] * ramp)))
        for q, value in enumerate((*third, *second)):
            out = jnp.where(out_lane == g * 4 + q, value, out)
    out_ref[...] = out


def inner_sums(x, dy, log_rate, rotation):
    steps, width = x.shape
    modes = log_rate.shape[0]
    groups = max(1, width // GROUP_W)
    chunks = steps // CHUNK
    state = jax.ShapeDtypeStruct((2 * modes, width), f32)
    vmem = pl.BlockSpec(memory_space=pltpu.VMEM)
    hbm = pl.BlockSpec(memory_space=pl.ANY)
    return pl.pallas_call(
        inner_kernel,
        in_specs=[hbm, hbm, vmem, vmem],
        out_specs=[vmem] * 3,
        out_shape=[jax.ShapeDtypeStruct((modes, LANES), f32), state, state],
        scratch_shapes=[
            pltpu.VMEM((steps, width), bf16),
            pltpu.VMEM((steps, width), bf16),
            pltpu.VMEM((groups, 8 * modes, L), bf16),
            pltpu.VMEM((groups, 8 * modes, L), bf16),
            pltpu.VMEM((groups, L, L), f32),
            pltpu.VMEM((4 * modes, width), f32),
            pltpu.VMEM((4 * modes, width), f32),
            pltpu.SemaphoreType.DMA((2, chunks)),
        ],
        cost_estimate=pl.CostEstimate(
            flops=6 * L * steps * width, bytes_accessed=4 * steps * width, transcendentals=0
        ),
        name="inner_sums",
    )(x, dy, log_rate, rotation)


def cross_kernel(n, copies, steps, lr_ref, ro_ref, rr_ref, ri_ref, in_ref, e_ref, xp_ref, yp_ref, skip_ref, *refs):
    received = refs[: n - 1]
    send_ref, exit_ref, total_ref, enter, late = refs[n - 1 :]
    modes, width = lr_ref.shape[0], e_ref.shape[1]
    share = min(width, GROUP_W)
    groups = width // share
    tiles = width // LANES
    m2 = 2 * modes
    me = lax.axis_index("ctx")
    base = first_group(width)
    direct = skip_ref[...]
    for r in received:
        direct = direct + r[tiles * m2 :, :]
    total_ref[...] = direct
    own = in_ref[...]
    row = lax.broadcasted_iota(jnp.int32, (modes, send_ref.shape[1]), 0)
    lane = lax.broadcasted_iota(jnp.int32, (modes, send_ref.shape[1]), 1)
    out = jnp.zeros(row.shape, f32)
    for g in range(groups):
        rate = jnp.exp(group_column(lr_ref, base + g))
        angle = group_column(ro_ref, base + g)
        real = group_column(rr_ref, base + g)
        imag = group_column(ri_ref, base + g)
        leap = powers(rate, angle, float(steps))
        leaps = [(jnp.ones_like(rate), jnp.zeros_like(rate))]
        for s in range(n - 2):
            leaps.append(cmul(leaps[-1], leap))
        third = [jnp.zeros((modes, LANES), f32)] * 2
        second = [jnp.zeros((modes, LANES), f32)] * 2
        for t in range(g * share // LANES, (g + 1) * share // LANES):
            cols = slice(t * LANES, (t + 1) * LANES)
            zero = jnp.zeros((modes, LANES), f32)
            entry, exit_, drift = (zero, zero), (zero, zero), (zero, zero)
            for s in range(1, n):
                got = received[s - 1]
                value = got[t * m2 : t * m2 + modes, :], got[t * m2 + modes : (t + 1) * m2, :]
                earlier = me - s >= 0
                from_past = cmul(leaps[s - 1], value)
                from_future = cmul(conj(leaps[n - s - 1]), value)
                entry = add(entry, [jnp.where(earlier, v, 0.0) for v in from_past])
                kept = [jnp.where(earlier, 0.0, v) for v in from_future]
                exit_ = add(exit_, kept)
                drift = add(drift, scale(float(steps * (n - s - 1)), kept))
            exit_ref[0:modes, cols] = exit_[0]
            exit_ref[modes:m2, cols] = exit_[1]
            e = e_ref[0:modes, cols], e_ref[modes:m2, cols]
            xp = xp_ref[0:modes, cols], xp_ref[modes:m2, cols]
            yp = yp_ref[0:modes, cols], yp_ref[modes:m2, cols]
            third = add(third, cdot(e, exit_))
            second = add(second, add(add(cdot(xp, exit_), cdot(e, drift)), cdot(entry, yp)))
        step = powers(rate, angle, 1.0)
        third = cmul(conj(step), (lane_sum(third[0]), lane_sum(third[1])))
        third = add(third, (own[:, g * 4 : g * 4 + 1], own[:, g * 4 + 1 : g * 4 + 2]))
        second = lane_sum(second[0]), lane_sum(second[1])
        second = add(second, (own[:, g * 4 + 2 : g * 4 + 3], own[:, g * 4 + 3 : g * 4 + 4]))
        decay = 1.0 - jnp.exp(-2.0 * rate)
        gain = jnp.sqrt(small_expm1(rate, decay))
        first = scale(gain, third)
        second = scale(gain, second)
        twist = cdot((real, imag), second)
        gain_term = real * third[0] + imag * third[1]
        pulled = cdot(twist, step)
        slope = jnp.exp(-2.0 * rate) / gain
        grads = (rate * (slope * gain_term - pulled[0]), -pulled[1], first[0], first[1])
        for q, value in enumerate(grads):
            out = jnp.where(lane == (g * 4 + q) * modes + row, value, out)
    line = jnp.sum(out, axis=0, keepdims=True)
    send_ref[...] = jnp.broadcast_to(line, send_ref.shape)


def small_expm1(rate, decay):
    z = 2.0 * rate
    terms = 8
    series = jnp.ones_like(z)
    for k in range(terms, 1, -1):
        series = 1.0 - z / k * series
    return jnp.where(z < 0.5, z * series, decay)


def cross_terms(n, devices, steps, params, own, e, xp, yp, skip, received):
    modes, width = params[0].shape[0], e.shape[1]
    groups = max(1, width // GROUP_W)
    line = -(-groups * 4 * modes // LANES) * LANES
    vmem = pl.BlockSpec(memory_space=pltpu.VMEM)
    return pl.pallas_call(
        functools.partial(cross_kernel, n, devices, steps),
        in_specs=[vmem] * (9 + n - 1),
        out_specs=[vmem] * 3,
        out_shape=[
            jax.ShapeDtypeStruct((devices, line), f32),
            jax.ShapeDtypeStruct(e.shape, f32),
            jax.ShapeDtypeStruct(skip.shape, f32),
        ],
        scratch_shapes=[pltpu.VMEM(e.shape, f32), pltpu.VMEM(e.shape, f32)],
        name="cross_terms",
    )(*params, own, e, xp, yp, skip, *received)


def input_kernel(dy_hbm, exit_ref, lr_ref, ro_ref, rr_ref, ri_ref, skip_ref, out_hbm, dy_buf, out_buf, near, pull, state, sem):
    steps, width = dy_hbm.shape
    modes = lr_ref.shape[0]
    share = min(width, GROUP_W)
    groups = width // share
    chunks = steps // CHUNK
    per = CHUNK // L
    copies = []
    for c in range(chunks):
        rows = pl.ds(c * CHUNK, CHUNK)
        copies.append(pltpu.make_async_copy(dy_hbm.at[rows], dy_buf.at[rows], sem.at[0, c]))
    for c in reversed(range(chunks)):
        copies[c].start()
    base = first_group(width)
    offset = positions(modes)
    row = lax.broadcasted_iota(jnp.int32, (L, L), 0)
    lane = lax.broadcasted_iota(jnp.int32, (L, L), 1)
    m2 = 2 * modes
    coeffs = []
    for g in range(groups):
        rate = jnp.exp(group_column(lr_ref, base + g))
        angle = group_column(ro_ref, base + g)
        real = group_column(rr_ref, base + g)
        imag = group_column(ri_ref, base + g)
        gain = jnp.sqrt(small_expm1(rate, 1.0 - jnp.exp(-2.0 * rate)))
        ahead = powers(rate, angle, offset)
        lags = jnp.sum(gain * (real * ahead[0] - imag * ahead[1]), axis=0, keepdims=True)
        rows = jnp.broadcast_to(lags, (L, L))
        bit = 1
        while bit < L:
            rows = jnp.where((row & bit) != 0, pltpu.roll(rows, bit, 1), rows)
            bit *= 2
        near[g, 0:L, :] = jnp.where(lane >= row, rows, 0.0).astype(bf16)
        near[g, L:, :] = split(conj(ahead))
        far = powers(rate, angle, float(L) - offset)
        pulls = [gain * (real * far[0] - imag * far[1]), gain * (real * far[1] + imag * far[0])]
        table = jnp.concatenate(pulls + pulls + [jnp.zeros((LANES - 2 * m2, L), f32)], axis=0)
        pull[g] = table.T[:, : 2 * m2].astype(bf16)
        coeffs.append(powers(rate, angle, float(L)))
    state[...] = exit_ref[...]
    outs = []
    for c in reversed(range(chunks)):
        copies[c].wait()
        for b in reversed(range(c * per, (c + 1) * per)):
            rows = slice(b * L, (b + 1) * L)
            for g in range(groups):
                cols = slice(g * share, (g + 1) * share)
                leap = coeffs[g]
                a = state[0:modes, cols], state[modes:m2, cols]
                yb = dy_buf[rows, cols]
                both = dot(near[g], yb)
                far = dot(pull[g], split(a))
                out_buf[rows, cols] = (both[:L] + far + skip_ref[:, cols] * yb.astype(f32)).astype(bf16)
                ys = both[L : L + m2] + both[L + m2 :]
                a = add(cmul(conj(leap), a), (ys[:modes], ys[modes:]))
                state[0:modes, cols], state[modes:m2, cols] = a
        rows = pl.ds(c * CHUNK, CHUNK)
        copy = pltpu.make_async_copy(out_buf.at[rows], out_hbm.at[rows], sem.at[1, c])
        copy.start()
        outs.append(copy)
    for copy in outs:
        copy.wait()


def input_grad(dy, exit_state, params, skip_gain):
    steps, width = dy.shape
    modes = params[0].shape[0]
    groups = max(1, width // GROUP_W)
    chunks = steps // CHUNK
    vmem = pl.BlockSpec(memory_space=pltpu.VMEM)
    hbm = pl.BlockSpec(memory_space=pl.ANY)
    return pl.pallas_call(
        input_kernel,
        in_specs=[hbm] + [vmem] * 6,
        out_specs=hbm,
        out_shape=jax.ShapeDtypeStruct((steps, width), bf16),
        scratch_shapes=[
            pltpu.VMEM((steps, width), bf16),
            pltpu.VMEM((steps, width), bf16),
            pltpu.VMEM((groups, L + 4 * modes, L), bf16),
            pltpu.VMEM((groups, L, 4 * modes), bf16),
            pltpu.VMEM((2 * modes, width), f32),
            pltpu.SemaphoreType.DMA((2, chunks)),
        ],
        cost_estimate=pl.CostEstimate(
            flops=4 * L * steps * width, bytes_accessed=4 * steps * width, transcendentals=0
        ),
        name="input_grad",
    )(dy, exit_state, *params, skip_gain)


def total_kernel(parts, width, in_ref, *outs):
    devices, line = in_ref.shape
    columns = devices // parts
    modes, groups = outs[0].shape
    local_groups = max(1, width // GROUP_W)
    table = in_ref[...]
    total = table[0:columns]
    for p in range(1, parts):
        total = total + table[p * columns : (p + 1) * columns]
    pad = -(-columns // LANES) * LANES - columns
    if pad:
        total = jnp.concatenate([total, jnp.zeros((pad, line), f32)], axis=0)
    turned = total.T
    source = lax.broadcasted_iota(jnp.int32, (columns + pad, groups), 0)
    group = lax.broadcasted_iota(jnp.int32, (columns + pad, groups), 1)
    for q in range(4):
        result = jnp.zeros((modes, groups), f32)
        for g in range(local_groups):
            start = (g * 4 + q) * modes
            place = (source * width // GROUP_W + g == group).astype(f32)
            result = result + jnp.dot(
                turned[start : start + modes, :],
                place,
                precision=lax.Precision.HIGHEST,
                preferred_element_type=f32,
            )
        outs[q][...] = result


def totals(parts, width, shape, gathered):
    vmem = pl.BlockSpec(memory_space=pltpu.VMEM)
    return pl.pallas_call(
        functools.partial(total_kernel, parts, width),
        in_specs=[vmem],
        out_specs=[vmem] * 4,
        out_shape=[jax.ShapeDtypeStruct(shape, f32)] * 4,
        name="totals",
    )(gathered)


def local(x, dy, log_rate, rotation, res_re, res_im, skip_gain):
    steps, width = x.shape
    n = lax.axis_size("ctx")
    devices = n * lax.axis_size("ch")
    params = (log_rate, rotation, res_re, res_im)
    *sends, e, y, skip = shard_sums(n, x, dy, log_rate, rotation)
    received = [
        lax.ppermute(part, "ctx", [(i, (i + s) % n) for i in range(n)])
        for s, part in enumerate(sends, 1)
    ]
    own, xp, yp = inner_sums(x, dy, log_rate, rotation)
    line, exit_state, direct = cross_terms(n, devices, steps, params, own, e, xp, yp, skip, received)
    gathered = lax.all_to_all(line, ("ctx", "ch"), 0, 0, tiled=True)
    grad_input = input_grad(dy, exit_state, params, skip_gain.reshape(1, width))
    grads = totals(n, width, log_rate.shape, gathered)
    return (grad_input, *grads, direct[: width // LANES].reshape(width))


def solution(mesh):
    placed = (P("ctx", "ch"), P("ctx", "ch"), P(), P(), P(), P(), P("ch"))
    return jax.shard_map(
        local,
        mesh=mesh,
        in_specs=placed,
        out_specs=(P("ctx", "ch"), P(), P(), P(), P(), P("ch")),
        check_vma=False,
    )
```

```python
import functools

import jax
import jax.numpy as jnp
from jax import lax
from jax.experimental import pallas as pl
from jax.experimental.pallas import tpu as pltpu
from jax.sharding import PartitionSpec as P

GROUP_W = 512
L = 256
CHUNK = 512

f32 = jnp.float32
bf16 = jnp.bfloat16
LANES = 128
SCOPED = 26 << 20


def dot(a, b):
    return jnp.dot(a, b, preferred_element_type=f32)


def group_column(ref, group):
    table = ref[...]
    lane = lax.broadcasted_iota(jnp.int32, table.shape, 1)
    return jnp.sum(jnp.where(lane == group, table, 0.0), axis=1, keepdims=True)


def powers(rate, angle, steps):
    magnitude = jnp.exp(-steps * rate)
    phase = steps * angle
    return magnitude * jnp.cos(phase), magnitude * jnp.sin(phase)


def cmul(a, b):
    return a[0] * b[0] - a[1] * b[1], a[0] * b[1] + a[1] * b[0]


def conj(a):
    return a[0], -a[1]


def cdot(a, b):
    return a[0] * b[0] + a[1] * b[1], a[0] * b[1] - a[1] * b[0]


def add(a, b):
    return a[0] + b[0], a[1] + b[1]


def scale(s, a):
    return s * a[0], s * a[1]


def split(parts):
    lead = [p.astype(bf16) for p in parts]
    rest = [(p - h.astype(f32)).astype(bf16) for p, h in zip(parts, lead)]
    return jnp.concatenate(lead + rest, axis=0)


def positions(modes):
    return lax.broadcasted_iota(jnp.int32, (modes, L), 1).astype(f32)


def first_group(width):
    return lax.axis_index("ch") * width // GROUP_W


def lane_sum(a):
    return jnp.sum(a, axis=1, keepdims=True)


def sums_kernel(n, x_hbm, dy_hbm, lr_hbm, ro_hbm, *refs):
    sends = refs[: n - 1]
    e_ref, skip_ref, x_buf, dy_buf, y_ref, lr_ref, ro_ref, tx, ty, sem, small = refs[n - 1 :]
    steps, width = x_hbm.shape
    early = (
        pltpu.make_async_copy(lr_hbm, lr_ref, small.at[0]),
        pltpu.make_async_copy(ro_hbm, ro_ref, small.at[1]),
    )
    for copy in early:
        copy.start()
    modes = lr_ref.shape[0]
    share = min(width, GROUP_W)
    groups = width // share
    chunks = steps // CHUNK
    m2 = 2 * modes
    copies = []
    for c in range(chunks):
        rows = pl.ds(c * CHUNK, CHUNK)
        pair = (
            pltpu.make_async_copy(x_hbm.at[rows], x_buf.at[rows], sem.at[0, c]),
            pltpu.make_async_copy(dy_hbm.at[rows], dy_buf.at[rows], sem.at[1, c]),
        )
        for copy in pair:
            copy.start(priority=1)
        copies.append(pair)
    for copy in early:
        copy.wait()
    base = first_group(width)
    offset = positions(modes)
    jumps = []
    for g in range(groups):
        rate = jnp.exp(group_column(lr_ref, base + g))
        angle = group_column(ro_ref, base + g)
        leap = powers(rate, angle, float(L))
        jumps.append(powers(rate, angle, float(CHUNK)))
        back = powers(rate, angle, (L - 1.0) - offset)
        ahead = conj(powers(rate, angle, offset))
        for b in range(CHUNK // L):
            tx[g, :, pl.ds(CHUNK - (b + 1) * L, L)] = split(back)
            ty[g, :, pl.ds(b * L, L)] = split(ahead)
            back = cmul(back, leap)
            ahead = cmul(ahead, conj(leap))
    reach = [(jnp.ones_like(jumps[0][0]), jnp.zeros_like(jumps[0][0]))] * groups
    direct = jnp.zeros((8, width), f32)
    for c in range(chunks):
        rows = slice(c * CHUNK, (c + 1) * CHUNK)
        for copy in copies[c]:
            copy.wait()
        for g in range(groups):
            cols = slice(g * share, (g + 1) * share)
            fwd = dot(tx[g], x_buf[rows, cols])
            bwd = dot(ty[g], dy_buf[rows, cols])
            fwd = fwd[:m2] + fwd[m2:]
            bwd = bwd[:m2] + bwd[m2:]
            e = fwd[:modes], fwd[modes:]
            y = bwd[:modes], bwd[modes:]
            if c > 0:
                e = add(e, cmul(jumps[g], (e_ref[:modes, cols], e_ref[modes:, cols])))
                reach[g] = cmul(reach[g], conj(jumps[g]))
                y = add(cmul(reach[g], y), (y_ref[:modes, cols], y_ref[modes:, cols]))
            e_ref[:modes, cols], e_ref[modes:, cols] = e
            y_ref[:modes, cols], y_ref[modes:, cols] = y
        prod = x_buf[rows, :].astype(f32) * dy_buf[rows, :].astype(f32)
        direct = direct + jnp.sum(prod.reshape(CHUNK // 8, 8, width), axis=0)
    total = jnp.sum(direct, axis=0, keepdims=True)
    me = lax.axis_index("ctx")
    e_all = e_ref[...]
    y_all = y_ref[...]
    tiles = width // LANES
    for t in range(tiles):
        skip_ref[t : t + 1, :] = total[:, t * LANES : (t + 1) * LANES]
    if tiles < 8:
        skip_ref[tiles:8, :] = jnp.zeros((8 - tiles, LANES), f32)
    for s in range(1, n):
        out = sends[s - 1]
        forward = me + s < n
        chosen = jnp.where(forward, e_all, y_all)
        for t in range(tiles):
            out[t * 2 * modes : (t + 1) * 2 * modes, :] = chosen[:, t * LANES : (t + 1) * LANES]
        out[tiles * 2 * modes :, :] = skip_ref[...]


def shard_sums(n, x, dy, log_rate, rotation):
    steps, width = x.shape
    modes = log_rate.shape[0]
    groups = max(1, width // GROUP_W)
    chunks = steps // CHUNK
    tiles = width // LANES
    extra = max(8, tiles)
    packed = jax.ShapeDtypeStruct((tiles * 2 * modes + extra, LANES), f32)
    state = jax.ShapeDtypeStruct((2 * modes, width), f32)
    vmem = pl.BlockSpec(memory_space=pltpu.VMEM)
    hbm = pl.BlockSpec(memory_space=pltpu.HBM)
    return pl.pallas_call(
        functools.partial(sums_kernel, n),
        in_specs=[hbm] * 4,
        out_specs=[vmem] * (n + 3),
        out_shape=[packed] * (n - 1)
        + [state, jax.ShapeDtypeStruct((extra, LANES), f32)]
        + [pltpu.VMEM((steps, width), bf16)] * 2,
        scratch_shapes=[
            pltpu.VMEM((2 * modes, width), f32),
            pltpu.VMEM(log_rate.shape, f32),
            pltpu.VMEM(log_rate.shape, f32),
            pltpu.VMEM((groups, 4 * modes, CHUNK), bf16),
            pltpu.VMEM((groups, 4 * modes, CHUNK), bf16),
            pltpu.SemaphoreType.DMA((2, chunks)),
            pltpu.SemaphoreType.DMA((2,)),
        ],
        cost_estimate=pl.CostEstimate(
            flops=8 * modes * steps * width * 2, bytes_accessed=4 * steps * width, transcendentals=0
        ),
        compiler_params=pltpu.CompilerParams(vmem_limit_bytes=SCOPED),
        name="shard_sums",
    )(*(pltpu.with_memory_space_constraint(a, pltpu.HBM) for a in (x, dy, log_rate, rotation)))


def inner_kernel(n, x_buf, dy_buf, lr_ref, ro_ref, rr_ref, ri_ref, *refs):
    out_ref, coef_ref, xp_ref, yp_ref, blk_ref, table_ref, tx, ty, corr, state, acc = refs
    steps, width = x_buf.shape
    modes = lr_ref.shape[0]
    share = min(width, GROUP_W)
    groups = width // share
    blocks = steps // L
    base = first_group(width)
    offset = positions(modes)
    row = lax.broadcasted_iota(jnp.int32, (L, L), 0)
    lane = lax.broadcasted_iota(jnp.int32, (L, L), 1)
    out_lane = lax.broadcasted_iota(jnp.int32, (modes, LANES), 1)
    m2, m3, m4 = 2 * modes, 3 * modes, 4 * modes
    coeffs = []
    for g in range(groups):
        rate = jnp.exp(group_column(lr_ref, base + g))
        angle = group_column(ro_ref, base + g)
        real = group_column(rr_ref, base + g)
        imag = group_column(ri_ref, base + g)
        decay = jnp.exp(-2.0 * rate)
        gain = jnp.sqrt(complement(rate, decay))
        leap = powers(rate, angle, float(L))
        behind = (L - 1.0) - offset
        back = powers(rate, angle, behind)
        ahead = powers(rate, angle, offset)
        lags = jnp.sum(gain * (real * ahead[0] - imag * ahead[1]), axis=0, keepdims=True)
        ahead = conj(ahead)
        tx[g] = split([*back, *scale(behind, back)])
        ty[g] = split([*ahead, *scale(offset + 1.0, ahead)])
        rows = jnp.broadcast_to(lags, (L, L))
        bit = 1
        while bit < L:
            rows = jnp.where((row & bit) != 0, pltpu.roll(rows, bit, 1), rows)
            bit *= 2
        table_ref[g, :, :L] = jnp.where(lane >= row, rows, 0.0).astype(bf16)
        far = powers(rate, angle, float(L) - offset)
        pulls = [gain * (real * far[0] - imag * far[1]), gain * (real * far[1] + imag * far[0])]
        pulls = pulls + pulls + [jnp.zeros((LANES - m4, L), f32)]
        table_ref[g, :, L:] = jnp.concatenate(pulls, axis=0).T[:, :m4].astype(bf16)
        step = powers(rate, angle, 1.0)
        coeffs.append((rate, angle, leap, ahead, step))
        whole = powers(rate, angle, float(steps))
        column = [real, imag, rate, gain, decay / gain, *step, *leap]
        power = (jnp.ones_like(rate), jnp.zeros_like(rate))
        for s in range(n - 1):
            column += power
            power = cmul(power, whole)
        table = jnp.zeros((modes, LANES), f32)
        for k, value in enumerate(column):
            table = jnp.where(out_lane == k, value, table)
        coef_ref[g] = table
    state[...] = jnp.zeros_like(state)
    acc[...] = jnp.zeros_like(acc)
    yp_ref[...] = jnp.zeros_like(yp_ref)
    corr[...] = jnp.zeros_like(corr)
    reach = [(jnp.ones_like(coeffs[0][0]), jnp.zeros_like(coeffs[0][0]))] * groups
    for b in range(blocks):
        rows = slice(b * L, (b + 1) * L)
        for g in range(groups):
            leap = coeffs[g][2]
            cols = slice(g * share, (g + 1) * share)
            xb = x_buf[rows, cols]
            yb = dy_buf[rows, cols]
            corr[g] += lax.dot_general(xb, yb, (((1,), (1,)), ((), ())), preferred_element_type=f32)
            xs = dot(tx[g], xb)
            xs = xs[:m4] + xs[m4:]
            ys = dot(ty[g], yb)
            ys = ys[:m4] + ys[m4:]
            blk_ref[b * m2 : (b + 1) * m2, cols] = ys[:m2]
            x0, x1 = (xs[:modes], xs[modes:m2]), (xs[m2:m3], xs[m3:])
            y0, y1 = (ys[:modes], ys[modes:m2]), (ys[m2:m3], ys[m3:])
            e = state[0:modes, cols], state[modes:m2, cols]
            ep = state[m2:m3, cols], state[m3:m4, cols]
            third = cdot(e, y0)
            second = add(cdot(ep, y0), cdot(e, y1))
            acc[0:modes, cols] += third[0]
            acc[modes:m2, cols] += third[1]
            acc[m2:m3, cols] += second[0]
            acc[m3:m4, cols] += second[1]
            ep = add(cmul(leap, add(ep, scale(float(L), e))), x1)
            e = add(cmul(leap, e), x0)
            state[0:modes, cols], state[modes:m2, cols] = e
            state[m2:m3, cols], state[m3:m4, cols] = ep
            far = add(y1, scale(float(b * L), y0))
            far = cmul(conj(reach[g]), far)
            yp_ref[0:modes, cols] += far[0]
            yp_ref[modes:m2, cols] += far[1]
            reach[g] = cmul(reach[g], leap)
    xp_ref[...] = state[m2:m4, :]
    out = jnp.zeros((modes, LANES), f32)
    for g in range(groups):
        rate, angle, leap, ahead, step = coeffs[g]
        cols = slice(g * share, (g + 1) * share)
        lagged = jnp.where(lane >= row, corr[g], 0.0)
        bit = 1
        while bit < L:
            lagged = jnp.where((row & bit) != 0, pltpu.roll(lagged, L - bit, 1), lagged)
            bit *= 2
        lags = jnp.sum(lagged, axis=0, keepdims=True)
        third = cmul(conj(step), (lane_sum(acc[0:modes, cols]), lane_sum(acc[modes:m2, cols])))
        second = lane_sum(acc[m2:m3, cols]), lane_sum(acc[m3:m4, cols])
        third = add(third, (lane_sum(ahead[0] * lags), lane_sum(ahead[1] * lags)))
        prior = conj(powers(rate, angle, jnp.maximum(offset - 1.0, 0.0)))
        ramp = offset * lags
        second = add(second, (lane_sum(prior[0] * ramp), lane_sum(prior[1] * ramp)))
        for q, value in enumerate((*third, *second)):
            out = jnp.where(out_lane == g * 4 + q, value, out)
    out_ref[...] = out


def complement(rate, decay):
    z = 2.0 * rate
    series = jnp.ones_like(z)
    for k in range(8, 1, -1):
        series = 1.0 - z / k * series
    return jnp.where(z < 0.5, z * series, 1.0 - decay)


def inner_sums(n, x, dy, params):
    steps, width = x.shape
    modes = params[0].shape[0]
    groups = max(1, width // GROUP_W)
    state = jax.ShapeDtypeStruct((2 * modes, width), f32)
    vmem = pl.BlockSpec(memory_space=pltpu.VMEM)
    return pl.pallas_call(
        functools.partial(inner_kernel, n),
        in_specs=[vmem] * 6,
        out_specs=[vmem] * 6,
        out_shape=[
            jax.ShapeDtypeStruct((modes, LANES), f32),
            jax.ShapeDtypeStruct((groups, modes, LANES), f32),
            state,
            state,
            jax.ShapeDtypeStruct((steps // L * 2 * modes, width), f32),
            jax.ShapeDtypeStruct((groups, L, L + 4 * modes), bf16),
        ],
        scratch_shapes=[
            pltpu.VMEM((groups, 8 * modes, L), bf16),
            pltpu.VMEM((groups, 8 * modes, L), bf16),
            pltpu.VMEM((groups, L, L), f32),
            pltpu.VMEM((4 * modes, width), f32),
            pltpu.VMEM((4 * modes, width), f32),
        ],
        cost_estimate=pl.CostEstimate(
            flops=8 * L * steps * width, bytes_accessed=4 * steps * width, transcendentals=0
        ),
        compiler_params=pltpu.CompilerParams(vmem_limit_bytes=SCOPED),
        name="inner_sums",
    )(*(pltpu.with_memory_space_constraint(a, pltpu.VMEM) for a in (x, dy)), *params)


def cross_kernel(n, steps, in_ref, coef_ref, e_ref, xp_ref, yp_ref, skip_ref, *refs):
    received = refs[: n - 1]
    send_ref, exit_ref, total_ref = refs[n - 1 :]
    modes = in_ref.shape[0]
    width = e_ref.shape[1]
    share = min(width, GROUP_W)
    groups = width // share
    tiles = width // LANES
    m2 = 2 * modes
    me = lax.axis_index("ctx")
    direct = skip_ref[...]
    for r in received:
        direct = direct + r[tiles * m2 :, :]
    total_ref[...] = direct
    own = in_ref[...]
    row = lax.broadcasted_iota(jnp.int32, (modes, send_ref.shape[1]), 0)
    lane = lax.broadcasted_iota(jnp.int32, (modes, send_ref.shape[1]), 1)
    out = jnp.zeros(row.shape, f32)
    for g in range(groups):
        real, imag, rate, gain, slope = (coef_ref[g, :, k : k + 1] for k in range(5))
        step = coef_ref[g, :, 5:6], coef_ref[g, :, 6:7]
        past, future = [], []
        for s in range(1, n):
            earlier = me - s >= 0
            k, r = 9 + 2 * (s - 1), 9 + 2 * (n - s - 1)
            power = coef_ref[g, :, k : k + 1], coef_ref[g, :, k + 1 : k + 2]
            past.append([jnp.where(earlier, v, 0.0) for v in power])
            power = coef_ref[g, :, r : r + 1], -coef_ref[g, :, r + 1 : r + 2]
            future.append([jnp.where(earlier, 0.0, v) for v in power])
        third = [jnp.zeros((modes, LANES), f32)] * 2
        second = [jnp.zeros((modes, LANES), f32)] * 2
        for t in range(g * share // LANES, (g + 1) * share // LANES):
            cols = slice(t * LANES, (t + 1) * LANES)
            zero = jnp.zeros((modes, LANES), f32)
            entry, exit_, drift = (zero, zero), (zero, zero), (zero, zero)
            for s in range(1, n):
                got = received[s - 1]
                value = got[t * m2 : t * m2 + modes, :], got[t * m2 + modes : (t + 1) * m2, :]
                entry = add(entry, cmul(past[s - 1], value))
                term = cmul(future[s - 1], value)
                exit_ = add(exit_, term)
                drift = add(drift, scale(float(steps * (n - s - 1)), term))
            exit_ref[0:modes, cols] = exit_[0]
            exit_ref[modes:m2, cols] = exit_[1]
            e = e_ref[0:modes, cols], e_ref[modes:m2, cols]
            xp = xp_ref[0:modes, cols], xp_ref[modes:m2, cols]
            yp = yp_ref[0:modes, cols], yp_ref[modes:m2, cols]
            third = add(third, cdot(e, exit_))
            second = add(second, add(add(cdot(xp, exit_), cdot(e, drift)), cdot(entry, yp)))
        third = cmul(conj(step), (lane_sum(third[0]), lane_sum(third[1])))
        third = add(third, (own[:, g * 4 : g * 4 + 1], own[:, g * 4 + 1 : g * 4 + 2]))
        second = lane_sum(second[0]), lane_sum(second[1])
        second = add(second, (own[:, g * 4 + 2 : g * 4 + 3], own[:, g * 4 + 3 : g * 4 + 4]))
        first = scale(gain, third)
        second = scale(gain, second)
        twist = cdot((real, imag), second)
        gain_term = real * third[0] + imag * third[1]
        pulled = cdot(twist, step)
        grads = (rate * (slope * gain_term - pulled[0]), -pulled[1], first[0], first[1])
        for q, value in enumerate(grads):
            out = jnp.where(lane == (g * 4 + q) * modes + row, value, out)
    line = jnp.sum(out, axis=0, keepdims=True)
    send_ref[...] = jnp.broadcast_to(line, send_ref.shape)


def cross_terms(n, devices, steps, own, coef, e, xp, yp, skip, received):
    groups, modes = coef.shape[:2]
    line = -(-groups * 4 * modes // LANES) * LANES
    vmem = pl.BlockSpec(memory_space=pltpu.VMEM)
    return pl.pallas_call(
        functools.partial(cross_kernel, n, steps),
        in_specs=[vmem] * (6 + n - 1),
        out_specs=[vmem] * 3,
        out_shape=[
            jax.ShapeDtypeStruct((devices, line), f32),
            jax.ShapeDtypeStruct(e.shape, f32),
            jax.ShapeDtypeStruct(skip.shape, f32),
        ],
        compiler_params=pltpu.CompilerParams(vmem_limit_bytes=SCOPED),
        name="cross_terms",
    )(own, coef, e, xp, yp, skip, *received)


def input_kernel(dy_hbm, table_ref, blk_ref, exit_ref, coef_ref, skip_ref, out_hbm, both, out_buf, sem):
    steps, width = dy_hbm.shape
    modes = exit_ref.shape[0] // 2
    share = min(width, GROUP_W)
    groups = width // share
    blocks = steps // L
    m2 = 2 * modes
    copies = []
    for b in range(blocks):
        rows = pl.ds(b * L, L)
        copies.append(pltpu.make_async_copy(dy_hbm.at[rows], both.at[b, pl.ds(0, L)], sem.at[0, b]))
        copies[b].start()
    for g in range(groups):
        cols = slice(g * share, (g + 1) * share)
        leap = coef_ref[g, :, 7:8], -coef_ref[g, :, 8:9]
        a = exit_ref[0:modes, cols], exit_ref[modes:m2, cols]
        for b in reversed(range(blocks)):
            both[b, L:, cols] = split(a)
            own = blk_ref[b * m2 : b * m2 + modes, cols], blk_ref[b * m2 + modes : (b + 1) * m2, cols]
            a = add(cmul(leap, a), own)
    outs = []
    for b in range(blocks):
        copies[b].wait()
        rows = slice(b * L, (b + 1) * L)
        for g in range(groups):
            cols = slice(g * share, (g + 1) * share)
            direct = skip_ref[:, cols] * both[b, :L, cols].astype(f32)
            out_buf[rows, cols] = (dot(table_ref[g], both[b, :, cols]) + direct).astype(bf16)
        rows = pl.ds(b * L, L)
        outs.append(pltpu.make_async_copy(out_buf.at[rows], out_hbm.at[rows], sem.at[1, b]))
        outs[b].start()
    for copy in outs:
        copy.wait()


def input_grad(dy, table, blk, exit_state, coef, skip_gain):
    steps, width = dy.shape
    depth = table.shape[2]
    blocks = steps // L
    vmem = pl.BlockSpec(memory_space=pltpu.VMEM)
    hbm = pl.BlockSpec(memory_space=pltpu.HBM)
    return pl.pallas_call(
        input_kernel,
        in_specs=[hbm] + [vmem] * 5,
        out_specs=hbm,
        out_shape=jax.ShapeDtypeStruct((steps, width), bf16),
        scratch_shapes=[
            pltpu.VMEM((blocks, depth, width), bf16),
            pltpu.VMEM((steps, width), bf16),
            pltpu.SemaphoreType.DMA((2, blocks)),
        ],
        cost_estimate=pl.CostEstimate(
            flops=4 * L * steps * width, bytes_accessed=4 * steps * width, transcendentals=0
        ),
        compiler_params=pltpu.CompilerParams(vmem_limit_bytes=SCOPED),
        name="input_grad",
    )(pltpu.with_memory_space_constraint(dy, pltpu.HBM), table, blk, exit_state, coef, skip_gain)


def total_kernel(parts, width, in_ref, *outs):
    devices, line = in_ref.shape
    columns = devices // parts
    modes, groups = outs[0].shape
    local_groups = max(1, width // GROUP_W)
    table = in_ref[...]
    total = table[0:columns]
    for p in range(1, parts):
        total = total + table[p * columns : (p + 1) * columns]
    pad = -(-columns // LANES) * LANES - columns
    if pad:
        total = jnp.concatenate([total, jnp.zeros((pad, line), f32)], axis=0)
    turned = total.T
    group = lax.broadcasted_iota(jnp.int32, (modes, groups), 1)
    for q in range(4):
        result = jnp.zeros((modes, groups), f32)
        for c in range(columns):
            for g in range(local_groups):
                start = (g * 4 + q) * modes
                value = turned[start : start + modes, c : c + 1]
                place = group == c * width // GROUP_W + g
                result = result + jnp.where(place, value, 0.0)
        outs[q][...] = result


def totals(parts, width, shape, gathered):
    vmem = pl.BlockSpec(memory_space=pltpu.VMEM)
    return pl.pallas_call(
        functools.partial(total_kernel, parts, width),
        in_specs=[vmem],
        out_specs=[vmem] * 4,
        out_shape=[jax.ShapeDtypeStruct(shape, f32)] * 4,
        compiler_params=pltpu.CompilerParams(vmem_limit_bytes=SCOPED),
        name="totals",
    )(gathered)


def local(x, dy, log_rate, rotation, res_re, res_im, skip_gain):
    steps, width = x.shape
    n = lax.axis_size("ctx")
    devices = n * lax.axis_size("ch")
    params = (log_rate, rotation, res_re, res_im)
    *sends, e, skip, x_near, dy_near = shard_sums(n, x, dy, log_rate, rotation)
    received = [
        lax.ppermute(part, "ctx", [(i, (i + s) % n) for i in range(n)])
        for s, part in enumerate(sends, 1)
    ]
    own, coef, xp, yp, blk, table = inner_sums(n, x_near, dy_near, params)
    line, exit_state, direct = cross_terms(n, devices, steps, own, coef, e, xp, yp, skip, received)
    gathered = lax.all_to_all(line, ("ctx", "ch"), 0, 0, tiled=True)
    grad_input = input_grad(dy, table, blk, exit_state, coef, skip_gain.reshape(1, width))
    grads = totals(n, width, log_rate.shape, gathered)
    return (grad_input, *grads, direct[: width // LANES].reshape(width))


def solution(mesh):
    placed = (P("ctx", "ch"), P("ctx", "ch"), P(), P(), P(), P(), P("ch"))
    return jax.shard_map(
        local,
        mesh=mesh,
        in_specs=placed,
        out_specs=(P("ctx", "ch"), P(), P(), P(), P(), P("ch")),
        check_vma=False,
    )
```

```python
import functools

import jax
import jax.numpy as jnp
from jax import lax
from jax.experimental import pallas as pl
from jax.experimental.pallas import tpu as pltpu
from jax.sharding import PartitionSpec as P

GROUP_W = 512
L = 256
HALF = 128
HEAD = 4
CHUNK = 512

f32 = jnp.float32
bf16 = jnp.bfloat16
LANES = 128
SCOPED = 26 << 20


def dot(a, b):
    return jnp.dot(a, b, preferred_element_type=f32)


def group_column(ref, group):
    table = ref[...]
    lane = lax.broadcasted_iota(jnp.int32, table.shape, 1)
    return jnp.sum(jnp.where(lane == group, table, 0.0), axis=1, keepdims=True)


def powers(rate, angle, steps):
    magnitude = jnp.exp(-steps * rate)
    phase = steps * angle
    return magnitude * jnp.cos(phase), magnitude * jnp.sin(phase)


def cmul(a, b):
    return a[0] * b[0] - a[1] * b[1], a[0] * b[1] + a[1] * b[0]


def conj(a):
    return a[0], -a[1]


def cdot(a, b):
    return a[0] * b[0] + a[1] * b[1], a[0] * b[1] - a[1] * b[0]


def add(a, b):
    return a[0] + b[0], a[1] + b[1]


def scale(s, a):
    return s * a[0], s * a[1]


def split(parts):
    lead = [p.astype(bf16) for p in parts]
    rest = [(p - h.astype(f32)).astype(bf16) for p, h in zip(parts, lead)]
    return jnp.concatenate(lead + rest, axis=0)


def positions(modes):
    return lax.broadcasted_iota(jnp.int32, (modes, L), 1).astype(f32)


def first_group(width):
    return lax.axis_index("ch") * width // GROUP_W


def lane_sum(a):
    return jnp.sum(a, axis=1, keepdims=True)


def sums_kernel(n, x_hbm, dy_hbm, lr_hbm, ro_hbm, *refs):
    sends = refs[: n - 1]
    e_ref, skip_ref, x_buf, dy_buf, y_ref, lr_ref, ro_ref, tx, ty, sem, small = refs[n - 1 :]
    steps, width = x_hbm.shape
    early = (
        pltpu.make_async_copy(lr_hbm, lr_ref, small.at[0]),
        pltpu.make_async_copy(ro_hbm, ro_ref, small.at[1]),
    )
    for copy in early:
        copy.start()
    modes = lr_ref.shape[0]
    share = min(width, GROUP_W)
    groups = width // share
    chunks = steps // CHUNK
    m2 = 2 * modes
    copies = []
    for c in range(chunks):
        rows = pl.ds(c * CHUNK, CHUNK)
        pair = (
            pltpu.make_async_copy(x_hbm.at[rows], x_buf.at[rows], sem.at[0, c]),
            pltpu.make_async_copy(dy_hbm.at[rows], dy_buf.at[rows], sem.at[1, c]),
        )
        for copy in pair:
            copy.start(priority=1)
        copies.append(pair)
    for copy in early:
        copy.wait()
    base = first_group(width)
    offset = positions(modes)
    jumps = []
    for g in range(groups):
        rate = jnp.exp(group_column(lr_ref, base + g))
        angle = group_column(ro_ref, base + g)
        leap = powers(rate, angle, float(L))
        jumps.append(powers(rate, angle, float(CHUNK)))
        back = powers(rate, angle, (L - 1.0) - offset)
        ahead = conj(powers(rate, angle, offset))
        for b in range(CHUNK // L):
            tx[g, :, pl.ds(CHUNK - (b + 1) * L, L)] = split(back)
            ty[g, :, pl.ds(b * L, L)] = split(ahead)
            back = cmul(back, leap)
            ahead = cmul(ahead, conj(leap))
    reach = [(jnp.ones_like(jumps[0][0]), jnp.zeros_like(jumps[0][0]))] * groups
    direct = jnp.zeros((8, width), f32)
    for c in range(chunks):
        rows = slice(c * CHUNK, (c + 1) * CHUNK)
        for copy in copies[c]:
            copy.wait()
        for g in range(groups):
            cols = slice(g * share, (g + 1) * share)
            fwd = dot(tx[g], x_buf[rows, cols])
            bwd = dot(ty[g], dy_buf[rows, cols])
            fwd = fwd[:m2] + fwd[m2:]
            bwd = bwd[:m2] + bwd[m2:]
            e = fwd[:modes], fwd[modes:]
            y = bwd[:modes], bwd[modes:]
            if c > 0:
                e = add(e, cmul(jumps[g], (e_ref[:modes, cols], e_ref[modes:, cols])))
                reach[g] = cmul(reach[g], conj(jumps[g]))
                y = add(cmul(reach[g], y), (y_ref[:modes, cols], y_ref[modes:, cols]))
            e_ref[:modes, cols], e_ref[modes:, cols] = e
            y_ref[:modes, cols], y_ref[modes:, cols] = y
        prod = x_buf[rows, :].astype(f32) * dy_buf[rows, :].astype(f32)
        direct = direct + jnp.sum(prod.reshape(CHUNK // 8, 8, width), axis=0)
    total = jnp.sum(direct, axis=0, keepdims=True)
    me = lax.axis_index("ctx")
    e_all = e_ref[...]
    y_all = y_ref[...]
    tiles = width // LANES
    for t in range(tiles):
        skip_ref[t : t + 1, :] = total[:, t * LANES : (t + 1) * LANES]
    if tiles < 8:
        skip_ref[tiles:8, :] = jnp.zeros((8 - tiles, LANES), f32)
    for s in range(1, n):
        out = sends[s - 1]
        forward = me + s < n
        chosen = jnp.where(forward, e_all, y_all)
        for t in range(tiles):
            out[t * 2 * modes : (t + 1) * 2 * modes, :] = chosen[:, t * LANES : (t + 1) * LANES]
        out[tiles * 2 * modes :, :] = skip_ref[...]


def shard_sums(n, x, dy, log_rate, rotation):
    steps, width = x.shape
    modes = log_rate.shape[0]
    groups = max(1, width // GROUP_W)
    chunks = steps // CHUNK
    tiles = width // LANES
    extra = max(8, tiles)
    packed = jax.ShapeDtypeStruct((tiles * 2 * modes + extra, LANES), f32)
    state = jax.ShapeDtypeStruct((2 * modes, width), f32)
    vmem = pl.BlockSpec(memory_space=pltpu.VMEM)
    hbm = pl.BlockSpec(memory_space=pltpu.HBM)
    return pl.pallas_call(
        functools.partial(sums_kernel, n),
        in_specs=[hbm] * 4,
        out_specs=[vmem] * (n + 3),
        out_shape=[packed] * (n - 1)
        + [state, jax.ShapeDtypeStruct((extra, LANES), f32)]
        + [pltpu.VMEM((steps, width), bf16)] * 2,
        scratch_shapes=[
            pltpu.VMEM((2 * modes, width), f32),
            pltpu.VMEM(log_rate.shape, f32),
            pltpu.VMEM(log_rate.shape, f32),
            pltpu.VMEM((groups, 4 * modes, CHUNK), bf16),
            pltpu.VMEM((groups, 4 * modes, CHUNK), bf16),
            pltpu.SemaphoreType.DMA((2, chunks)),
            pltpu.SemaphoreType.DMA((2,)),
        ],
        cost_estimate=pl.CostEstimate(
            flops=8 * modes * steps * width * 2, bytes_accessed=4 * steps * width, transcendentals=0
        ),
        compiler_params=pltpu.CompilerParams(vmem_limit_bytes=SCOPED),
        name="shard_sums",
    )(*(pltpu.with_memory_space_constraint(a, pltpu.HBM) for a in (x, dy, log_rate, rotation)))


def inner_kernel(n, x_buf, dy_buf, lr_ref, ro_ref, rr_ref, ri_ref, *refs):
    out_ref, coef_ref, xp_ref, yp_ref, blk_ref, mid_ref, table_ref, head_ref, tx, ty, corr, state, acc = refs
    steps, width = x_buf.shape
    modes = lr_ref.shape[0]
    share = min(width, GROUP_W)
    groups = width // share
    blocks = steps // L
    base = first_group(width)
    offset = positions(modes)
    row = lax.broadcasted_iota(jnp.int32, (L, L), 0)
    lane = lax.broadcasted_iota(jnp.int32, (L, L), 1)
    out_lane = lax.broadcasted_iota(jnp.int32, (modes, LANES), 1)
    m2, m3, m4 = 2 * modes, 3 * modes, 4 * modes
    coeffs = []
    for g in range(groups):
        rate = jnp.exp(group_column(lr_ref, base + g))
        angle = group_column(ro_ref, base + g)
        real = group_column(rr_ref, base + g)
        imag = group_column(ri_ref, base + g)
        decay = jnp.exp(-2.0 * rate)
        gain = jnp.sqrt(complement(rate, decay))
        leap = powers(rate, angle, float(L))
        behind = (L - 1.0) - offset
        back = powers(rate, angle, behind)
        ahead = powers(rate, angle, offset)
        lags = jnp.sum(gain * (real * ahead[0] - imag * ahead[1]), axis=0, keepdims=True)
        ahead = conj(ahead)
        tx[g] = split([*back, *scale(behind, back)])
        later = conj(powers(rate, angle, jnp.maximum(offset - HALF, 0.0)))
        later = [jnp.where(offset >= HALF, part, 0.0) for part in later]
        ty[g, : 2 * m4, :] = split([*ahead, *scale(offset + 1.0, ahead)])
        ty[g, 2 * m4 :, :] = split(later)
        rows = jnp.broadcast_to(lags[:, :HALF], (HALF, HALF))
        bit = 1
        while bit < HALF:
            shifted = (row[:HALF, :HALF] & bit) != 0
            rows = jnp.where(shifted, pltpu.roll(rows, bit, 1), rows)
            bit *= 2
        upper = lane[:HALF, :HALF] >= row[:HALF, :HALF]
        table_ref[g, :, :HALF] = jnp.where(upper, rows, 0.0).astype(bf16)
        far = powers(rate, angle, float(HALF) - offset[:, :HALF])
        pulls = [gain * (real * far[0] - imag * far[1]), gain * (real * far[1] + imag * far[0])]
        pulls = pulls + pulls + [jnp.zeros((LANES - m4, HALF), f32)]
        table_ref[g, :, HALF:] = jnp.concatenate(pulls, axis=0).T[:, :m4].astype(bf16)
        half = powers(rate, angle, float(HALF))
        step = powers(rate, angle, 1.0)
        coeffs.append((rate, angle, leap, ahead, step))
        whole = powers(rate, angle, float(steps))
        column = [real, imag, rate, gain, decay / gain, *step, *leap, *half]
        power = (jnp.ones_like(rate), jnp.zeros_like(rate))
        for s in range(n - 1):
            column += power
            power = cmul(power, whole)
        table = jnp.zeros((modes, LANES), f32)
        for k, value in enumerate(column):
            table = jnp.where(out_lane == k, value, table)
        coef_ref[g] = table
    state[...] = jnp.zeros_like(state)
    acc[...] = jnp.zeros_like(acc)
    yp_ref[...] = jnp.zeros_like(yp_ref)
    corr[...] = jnp.zeros_like(corr)
    reach = [(jnp.ones_like(coeffs[0][0]), jnp.zeros_like(coeffs[0][0]))] * groups
    for b in range(blocks):
        rows = slice(b * L, (b + 1) * L)
        for g in range(groups):
            leap = coeffs[g][2]
            cols = slice(g * share, (g + 1) * share)
            xb = x_buf[rows, cols]
            yb = dy_buf[rows, cols]
            corr[g] += lax.dot_general(xb, yb, (((1,), (1,)), ((), ())), preferred_element_type=f32)
            xs = dot(tx[g], xb)
            xs = xs[:m4] + xs[m4:]
            ys = dot(ty[g], yb)
            mid = ys[2 * m4 : 2 * m4 + m2] + ys[2 * m4 + m2 :]
            mid_ref[b * m2 : (b + 1) * m2, cols] = mid.astype(bf16)
            ys = ys[:m4] + ys[m4 : 2 * m4]
            blk_ref[b * m2 : (b + 1) * m2, cols] = ys[:m2].astype(bf16)
            x0, x1 = (xs[:modes], xs[modes:m2]), (xs[m2:m3], xs[m3:])
            y0, y1 = (ys[:modes], ys[modes:m2]), (ys[m2:m3], ys[m3:])
            e = state[0:modes, cols], state[modes:m2, cols]
            ep = state[m2:m3, cols], state[m3:m4, cols]
            third = cdot(e, y0)
            second = add(cdot(ep, y0), cdot(e, y1))
            acc[0:modes, cols] += third[0]
            acc[modes:m2, cols] += third[1]
            acc[m2:m3, cols] += second[0]
            acc[m3:m4, cols] += second[1]
            ep = add(cmul(leap, add(ep, scale(float(L), e))), x1)
            e = add(cmul(leap, e), x0)
            state[0:modes, cols], state[modes:m2, cols] = e
            state[m2:m3, cols], state[m3:m4, cols] = ep
            far = add(y1, scale(float(b * L), y0))
            far = cmul(conj(reach[g]), far)
            yp_ref[0:modes, cols] += far[0]
            yp_ref[modes:m2, cols] += far[1]
            reach[g] = cmul(reach[g], leap)
    xp_ref[...] = state[m2:m4, :]
    head_ref[...] = dy_buf[: HEAD * HALF, :].reshape(head_ref.shape)
    out = jnp.zeros((modes, LANES), f32)
    for g in range(groups):
        rate, angle, leap, ahead, step = coeffs[g]
        cols = slice(g * share, (g + 1) * share)
        lagged = jnp.where(lane >= row, corr[g], 0.0)
        bit = 1
        while bit < L:
            lagged = jnp.where((row & bit) != 0, pltpu.roll(lagged, L - bit, 1), lagged)
            bit *= 2
        lags = jnp.sum(lagged, axis=0, keepdims=True)
        third = cmul(conj(step), (lane_sum(acc[0:modes, cols]), lane_sum(acc[modes:m2, cols])))
        second = lane_sum(acc[m2:m3, cols]), lane_sum(acc[m3:m4, cols])
        third = add(third, (lane_sum(ahead[0] * lags), lane_sum(ahead[1] * lags)))
        prior = conj(powers(rate, angle, jnp.maximum(offset - 1.0, 0.0)))
        ramp = offset * lags
        second = add(second, (lane_sum(prior[0] * ramp), lane_sum(prior[1] * ramp)))
        for q, value in enumerate((*third, *second)):
            out = jnp.where(out_lane == g * 4 + q, value, out)
    out_ref[...] = out


def complement(rate, decay):
    z = 2.0 * rate
    series = jnp.ones_like(z)
    for k in range(8, 1, -1):
        series = 1.0 - z / k * series
    return jnp.where(z < 0.5, z * series, 1.0 - decay)


def inner_sums(n, x, dy, params):
    steps, width = x.shape
    modes = params[0].shape[0]
    groups = max(1, width // GROUP_W)
    state = jax.ShapeDtypeStruct((2 * modes, width), f32)
    vmem = pl.BlockSpec(memory_space=pltpu.VMEM)
    return pl.pallas_call(
        functools.partial(inner_kernel, n),
        in_specs=[vmem] * 6,
        out_specs=[vmem] * 8,
        out_shape=[
            jax.ShapeDtypeStruct((modes, LANES), f32),
            jax.ShapeDtypeStruct((groups, modes, LANES), f32),
            state,
            state,
            jax.ShapeDtypeStruct((steps // L * 2 * modes, width), bf16),
            jax.ShapeDtypeStruct((steps // L * 2 * modes, width), bf16),
            jax.ShapeDtypeStruct((groups, HALF, HALF + 4 * modes), bf16),
            jax.ShapeDtypeStruct((HEAD, HALF, width), bf16),
        ],
        scratch_shapes=[
            pltpu.VMEM((groups, 8 * modes, L), bf16),
            pltpu.VMEM((groups, 12 * modes, L), bf16),
            pltpu.VMEM((groups, L, L), f32),
            pltpu.VMEM((4 * modes, width), f32),
            pltpu.VMEM((4 * modes, width), f32),
        ],
        cost_estimate=pl.CostEstimate(
            flops=8 * L * steps * width, bytes_accessed=4 * steps * width, transcendentals=0
        ),
        compiler_params=pltpu.CompilerParams(vmem_limit_bytes=SCOPED),
        name="inner_sums",
    )(*(pltpu.with_memory_space_constraint(a, pltpu.VMEM) for a in (x, dy)), *params)


def cross_kernel(n, steps, in_ref, coef_ref, e_ref, xp_ref, yp_ref, skip_ref, *refs):
    received = refs[: n - 1]
    send_ref, exit_ref, total_ref = refs[n - 1 :]
    modes = in_ref.shape[0]
    width = e_ref.shape[1]
    share = min(width, GROUP_W)
    groups = width // share
    tiles = width // LANES
    m2 = 2 * modes
    me = lax.axis_index("ctx")
    direct = skip_ref[...]
    for r in received:
        direct = direct + r[tiles * m2 :, :]
    total_ref[...] = direct
    own = in_ref[...]
    row = lax.broadcasted_iota(jnp.int32, (modes, send_ref.shape[1]), 0)
    lane = lax.broadcasted_iota(jnp.int32, (modes, send_ref.shape[1]), 1)
    out = jnp.zeros(row.shape, f32)
    for g in range(groups):
        real, imag, rate, gain, slope = (coef_ref[g, :, k : k + 1] for k in range(5))
        step = coef_ref[g, :, 5:6], coef_ref[g, :, 6:7]
        past, future = [], []
        for s in range(1, n):
            earlier = me - s >= 0
            k, r = 11 + 2 * (s - 1), 11 + 2 * (n - s - 1)
            power = coef_ref[g, :, k : k + 1], coef_ref[g, :, k + 1 : k + 2]
            past.append([jnp.where(earlier, v, 0.0) for v in power])
            power = coef_ref[g, :, r : r + 1], -coef_ref[g, :, r + 1 : r + 2]
            future.append([jnp.where(earlier, 0.0, v) for v in power])
        third = [jnp.zeros((modes, LANES), f32)] * 2
        second = [jnp.zeros((modes, LANES), f32)] * 2
        for t in range(g * share // LANES, (g + 1) * share // LANES):
            cols = slice(t * LANES, (t + 1) * LANES)
            zero = jnp.zeros((modes, LANES), f32)
            entry, exit_, drift = (zero, zero), (zero, zero), (zero, zero)
            for s in range(1, n):
                got = received[s - 1]
                value = got[t * m2 : t * m2 + modes, :], got[t * m2 + modes : (t + 1) * m2, :]
                entry = add(entry, cmul(past[s - 1], value))
                term = cmul(future[s - 1], value)
                exit_ = add(exit_, term)
                drift = add(drift, scale(float(steps * (n - s - 1)), term))
            exit_ref[0:modes, cols] = exit_[0]
            exit_ref[modes:m2, cols] = exit_[1]
            e = e_ref[0:modes, cols], e_ref[modes:m2, cols]
            xp = xp_ref[0:modes, cols], xp_ref[modes:m2, cols]
            yp = yp_ref[0:modes, cols], yp_ref[modes:m2, cols]
            third = add(third, cdot(e, exit_))
            second = add(second, add(add(cdot(xp, exit_), cdot(e, drift)), cdot(entry, yp)))
        third = cmul(conj(step), (lane_sum(third[0]), lane_sum(third[1])))
        third = add(third, (own[:, g * 4 : g * 4 + 1], own[:, g * 4 + 1 : g * 4 + 2]))
        second = lane_sum(second[0]), lane_sum(second[1])
        second = add(second, (own[:, g * 4 + 2 : g * 4 + 3], own[:, g * 4 + 3 : g * 4 + 4]))
        first = scale(gain, third)
        second = scale(gain, second)
        twist = cdot((real, imag), second)
        gain_term = real * third[0] + imag * third[1]
        pulled = cdot(twist, step)
        grads = (rate * (slope * gain_term - pulled[0]), -pulled[1], first[0], first[1])
        for q, value in enumerate(grads):
            out = jnp.where(lane == (g * 4 + q) * modes + row, value, out)
    line = jnp.sum(out, axis=0, keepdims=True)
    send_ref[...] = jnp.broadcast_to(line, send_ref.shape)


def cross_terms(n, devices, steps, own, coef, e, xp, yp, skip, received):
    groups, modes = coef.shape[:2]
    line = -(-groups * 4 * modes // LANES) * LANES
    vmem = pl.BlockSpec(memory_space=pltpu.VMEM)
    return pl.pallas_call(
        functools.partial(cross_kernel, n, steps),
        in_specs=[vmem] * (6 + n - 1),
        out_specs=[vmem] * 3,
        out_shape=[
            jax.ShapeDtypeStruct((devices, line), f32),
            jax.ShapeDtypeStruct(e.shape, f32),
            jax.ShapeDtypeStruct(skip.shape, f32),
        ],
        compiler_params=pltpu.CompilerParams(vmem_limit_bytes=SCOPED),
        name="cross_terms",
    )(own, coef, e, xp, yp, skip, *received)


def input_kernel(dy_hbm, head_ref, table_ref, blk_ref, mid_ref, exit_ref, coef_ref, skip_ref, *refs):
    out_hbm, both, out_buf, sem = refs
    blocks, _, width = dy_hbm.shape
    modes = exit_ref.shape[0] // 2
    share = min(width, GROUP_W)
    groups = width // share
    m2 = 2 * modes
    cuts = last_cuts(blocks)
    copies = []
    for c, (start, count) in enumerate(cuts):
        part = pl.ds(start, count)
        copy = None
        if c > 0:
            copy = pltpu.make_async_copy(dy_hbm.at[part], both.at[part, pl.ds(0, HALF)], sem.at[0, c])
            copy.start()
        copies.append(copy)
    both[:HEAD, :HALF, :] = head_ref[...]
    for g in range(groups):
        cols = slice(g * share, (g + 1) * share)
        leap = coef_ref[g, :, 7:8], -coef_ref[g, :, 8:9]
        half = coef_ref[g, :, 9:10], -coef_ref[g, :, 10:11]
        a = exit_ref[0:modes, cols], exit_ref[modes:m2, cols]
        for b in reversed(range(blocks // 2)):
            rows = slice(b * m2, (b + 1) * m2)
            both[2 * b + 1, HALF:, cols] = split(a)
            mid = mid_ref[rows, cols].astype(f32)
            both[2 * b, HALF:, cols] = split(add(cmul(half, a), (mid[:modes], mid[modes:])))
            own = blk_ref[rows, cols].astype(f32)
            a = add(cmul(leap, a), (own[:modes], own[modes:]))
    outs = []
    for c, (start, count) in enumerate(cuts):
        if c > 0:
            copies[c].wait()
        for b in range(start, start + count):
            for g in range(groups):
                cols = slice(g * share, (g + 1) * share)
                direct = skip_ref[:, cols] * both[b, :HALF, cols].astype(f32)
                out_buf[b, :, cols] = (dot(table_ref[g], both[b, :, cols]) + direct).astype(bf16)
        part = pl.ds(start, count)
        outs.append(pltpu.make_async_copy(out_buf.at[part], out_hbm.at[part], sem.at[1, c]))
        outs[c].start()
    for copy in outs:
        copy.wait()


def last_cuts(blocks):
    per = CHUNK // HALF
    starts = [0, *range(HEAD, blocks, per), blocks - per // 2, blocks]
    return [(a, b - a) for a, b in zip(starts, starts[1:])]


def input_grad(dy, head, table, blk, mid, exit_state, coef, skip_gain):
    steps, width = dy.shape
    depth = table.shape[2]
    blocks = steps // HALF
    vmem = pl.BlockSpec(memory_space=pltpu.VMEM)
    hbm = pl.BlockSpec(memory_space=pltpu.HBM)
    dy = pltpu.with_memory_space_constraint(dy.reshape(blocks, HALF, width), pltpu.HBM)
    out = pl.pallas_call(
        input_kernel,
        in_specs=[hbm] + [vmem] * 7,
        out_specs=hbm,
        out_shape=jax.ShapeDtypeStruct((blocks, HALF, width), bf16),
        scratch_shapes=[
            pltpu.VMEM((blocks, depth, width), bf16),
            pltpu.VMEM((blocks, HALF, width), bf16),
            pltpu.SemaphoreType.DMA((2, len(last_cuts(blocks)))),
        ],
        cost_estimate=pl.CostEstimate(
            flops=4 * HALF * steps * width, bytes_accessed=4 * steps * width, transcendentals=0
        ),
        compiler_params=pltpu.CompilerParams(vmem_limit_bytes=SCOPED),
        name="input_grad",
    )(dy, head, table, blk, mid, exit_state, coef, skip_gain)
    return out.reshape(steps, width)


def total_kernel(parts, width, in_ref, *outs):
    devices, line = in_ref.shape
    columns = devices // parts
    modes, groups = outs[0].shape
    local_groups = max(1, width // GROUP_W)
    table = in_ref[...]
    total = table[0:columns]
    for p in range(1, parts):
        total = total + table[p * columns : (p + 1) * columns]
    pad = -(-columns // LANES) * LANES - columns
    if pad:
        total = jnp.concatenate([total, jnp.zeros((pad, line), f32)], axis=0)
    turned = total.T
    group = lax.broadcasted_iota(jnp.int32, (modes, groups), 1)
    for q in range(4):
        result = jnp.zeros((modes, groups), f32)
        for c in range(columns):
            for g in range(local_groups):
                start = (g * 4 + q) * modes
                value = turned[start : start + modes, c : c + 1]
                place = group == c * width // GROUP_W + g
                result = result + jnp.where(place, value, 0.0)
        outs[q][...] = result


def totals(parts, width, shape, gathered):
    vmem = pl.BlockSpec(memory_space=pltpu.VMEM)
    return pl.pallas_call(
        functools.partial(total_kernel, parts, width),
        in_specs=[vmem],
        out_specs=[vmem] * 4,
        out_shape=[jax.ShapeDtypeStruct(shape, f32)] * 4,
        compiler_params=pltpu.CompilerParams(vmem_limit_bytes=SCOPED),
        name="totals",
    )(gathered)


def local(x, dy, log_rate, rotation, res_re, res_im, skip_gain):
    steps, width = x.shape
    n = lax.axis_size("ctx")
    devices = n * lax.axis_size("ch")
    params = (log_rate, rotation, res_re, res_im)
    *sends, e, skip, x_near, dy_near = shard_sums(n, x, dy, log_rate, rotation)
    received = [
        lax.ppermute(part, "ctx", [(i, (i + s) % n) for i in range(n)])
        for s, part in enumerate(sends, 1)
    ]
    own, coef, xp, yp, blk, mid, table, head = inner_sums(n, x_near, dy_near, params)
    line, exit_state, direct = cross_terms(n, devices, steps, own, coef, e, xp, yp, skip, received)
    gathered = lax.all_to_all(line, ("ctx", "ch"), 0, 0, tiled=True)
    grad_input = input_grad(
        dy, head, table, blk, mid, exit_state, coef, skip_gain.reshape(1, width)
    )
    grads = totals(n, width, log_rate.shape, gathered)
    return (grad_input, *grads, direct[: width // LANES].reshape(width))


def solution(mesh):
    placed = (P("ctx", "ch"), P("ctx", "ch"), P(), P(), P(), P(), P("ch"))
    return jax.shard_map(
        local,
        mesh=mesh,
        in_specs=placed,
        out_specs=(P("ctx", "ch"), P(), P(), P(), P(), P("ch")),
        check_vma=False,
    )
```

```python
import functools

import jax
import jax.numpy as jnp
from jax import lax
from jax.experimental import pallas as pl
from jax.experimental.pallas import tpu as pltpu
from jax.sharding import PartitionSpec as P

GROUP_W = 512
L = 256
HALF = 128
HEAD = 4
CHUNK = 512

f32 = jnp.float32
bf16 = jnp.bfloat16
LANES = 128
SCOPED = 26 << 20


def dot(a, b):
    return jnp.dot(a, b, preferred_element_type=f32)


def group_column(ref, group):
    table = ref[...]
    lane = lax.broadcasted_iota(jnp.int32, table.shape, 1)
    return jnp.sum(jnp.where(lane == group, table, 0.0), axis=1, keepdims=True)


def powers(rate, angle, steps):
    magnitude = jnp.exp(-steps * rate)
    phase = steps * angle
    return magnitude * jnp.cos(phase), magnitude * jnp.sin(phase)


def cmul(a, b):
    return a[0] * b[0] - a[1] * b[1], a[0] * b[1] + a[1] * b[0]


def conj(a):
    return a[0], -a[1]


def cdot(a, b):
    return a[0] * b[0] + a[1] * b[1], a[0] * b[1] - a[1] * b[0]


def add(a, b):
    return a[0] + b[0], a[1] + b[1]


def scale(s, a):
    return s * a[0], s * a[1]


def split(parts):
    lead = [p.astype(bf16) for p in parts]
    rest = [(p - h.astype(f32)).astype(bf16) for p, h in zip(parts, lead)]
    return jnp.concatenate(lead + rest, axis=0)


def positions(modes):
    return lax.broadcasted_iota(jnp.int32, (modes, L), 1).astype(f32)


def first_group(width):
    return lax.axis_index("ch") * width // GROUP_W


def lane_sum(a):
    return jnp.sum(a, axis=1, keepdims=True)


def sums_kernel(n, x_hbm, dy_hbm, lr_hbm, ro_hbm, *refs):
    sends = refs[: n - 1]
    e_ref, skip_ref, x_buf, dy_buf, y_ref, lr_ref, ro_ref, tx, ty, sem, small = refs[n - 1 :]
    steps, width = x_hbm.shape
    early = (
        pltpu.make_async_copy(lr_hbm, lr_ref, small.at[0]),
        pltpu.make_async_copy(ro_hbm, ro_ref, small.at[1]),
    )
    for copy in early:
        copy.start()
    modes = lr_ref.shape[0]
    share = min(width, GROUP_W)
    groups = width // share
    cuts = first_cuts(steps)
    m2 = 2 * modes
    copies = []
    for c, (start, count) in enumerate(cuts):
        rows = pl.ds(start, count)
        pair = (
            pltpu.make_async_copy(x_hbm.at[rows], x_buf.at[rows], sem.at[0, c]),
            pltpu.make_async_copy(dy_hbm.at[rows], dy_buf.at[rows], sem.at[1, c]),
        )
        for copy in pair:
            copy.start(priority=1)
        copies.append(pair)
    for copy in early:
        copy.wait()
    base = first_group(width)
    offset = positions(modes)
    jumps = []
    for g in range(groups):
        rate = jnp.exp(group_column(lr_ref, base + g))
        angle = group_column(ro_ref, base + g)
        leap = powers(rate, angle, float(L))
        jumps.append({k: powers(rate, angle, float(k)) for k in {count for _, count in cuts}})
        back = powers(rate, angle, (L - 1.0) - offset)
        ahead = conj(powers(rate, angle, offset))
        for b in range(CHUNK // L):
            tx[g, :, pl.ds(CHUNK - (b + 1) * L, L)] = split(back)
            ty[g, :, pl.ds(b * L, L)] = split(ahead)
            back = cmul(back, leap)
            ahead = cmul(ahead, conj(leap))
    reach = [None] * groups
    direct = jnp.zeros((8, width), f32)
    for c, (start, count) in enumerate(cuts):
        rows = slice(start, start + count)
        for copy in copies[c]:
            copy.wait()
        for g in range(groups):
            cols = slice(g * share, (g + 1) * share)
            fwd = dot(tx[g, :, CHUNK - count :], x_buf[rows, cols])
            bwd = dot(ty[g, :, :count], dy_buf[rows, cols])
            fwd = fwd[:m2] + fwd[m2:]
            bwd = bwd[:m2] + bwd[m2:]
            e = fwd[:modes], fwd[modes:]
            y = bwd[:modes], bwd[modes:]
            if c > 0:
                e = add(e, cmul(jumps[g][count], (e_ref[:modes, cols], e_ref[modes:, cols])))
                last = conj(jumps[g][cuts[c - 1][1]])
                reach[g] = last if c == 1 else cmul(reach[g], last)
                y = add(cmul(reach[g], y), (y_ref[:modes, cols], y_ref[modes:, cols]))
            e_ref[:modes, cols], e_ref[modes:, cols] = e
            y_ref[:modes, cols], y_ref[modes:, cols] = y
        prod = x_buf[rows, :].astype(f32) * dy_buf[rows, :].astype(f32)
        direct = direct + jnp.sum(prod.reshape(count // 8, 8, width), axis=0)
    total = jnp.sum(direct, axis=0, keepdims=True)
    me = lax.axis_index("ctx")
    e_all = e_ref[...]
    y_all = y_ref[...]
    tiles = width // LANES
    for t in range(tiles):
        skip_ref[t : t + 1, :] = total[:, t * LANES : (t + 1) * LANES]
    if tiles < 8:
        skip_ref[tiles:8, :] = jnp.zeros((8 - tiles, LANES), f32)
    for s in range(1, n):
        out = sends[s - 1]
        forward = me + s < n
        chosen = jnp.where(forward, e_all, y_all)
        for t in range(tiles):
            out[t * 2 * modes : (t + 1) * 2 * modes, :] = chosen[:, t * LANES : (t + 1) * LANES]
        out[tiles * 2 * modes :, :] = skip_ref[...]


def first_cuts(steps):
    starts = [*range(0, steps, CHUNK), steps - L, steps]
    return [(a, b - a) for a, b in zip(starts, starts[1:])]


def shard_sums(n, x, dy, log_rate, rotation):
    steps, width = x.shape
    modes = log_rate.shape[0]
    groups = max(1, width // GROUP_W)
    tiles = width // LANES
    extra = max(8, tiles)
    packed = jax.ShapeDtypeStruct((tiles * 2 * modes + extra, LANES), f32)
    state = jax.ShapeDtypeStruct((2 * modes, width), f32)
    vmem = pl.BlockSpec(memory_space=pltpu.VMEM)
    hbm = pl.BlockSpec(memory_space=pltpu.HBM)
    return pl.pallas_call(
        functools.partial(sums_kernel, n),
        in_specs=[hbm] * 4,
        out_specs=[vmem] * (n + 3),
        out_shape=[packed] * (n - 1)
        + [state, jax.ShapeDtypeStruct((extra, LANES), f32)]
        + [pltpu.VMEM((steps, width), bf16)] * 2,
        scratch_shapes=[
            pltpu.VMEM((2 * modes, width), f32),
            pltpu.VMEM(log_rate.shape, f32),
            pltpu.VMEM(log_rate.shape, f32),
            pltpu.VMEM((groups, 4 * modes, CHUNK), bf16),
            pltpu.VMEM((groups, 4 * modes, CHUNK), bf16),
            pltpu.SemaphoreType.DMA((2, len(first_cuts(steps)))),
            pltpu.SemaphoreType.DMA((2,)),
        ],
        cost_estimate=pl.CostEstimate(
            flops=8 * modes * steps * width * 2, bytes_accessed=4 * steps * width, transcendentals=0
        ),
        compiler_params=pltpu.CompilerParams(vmem_limit_bytes=SCOPED),
        name="shard_sums",
    )(*(pltpu.with_memory_space_constraint(a, pltpu.HBM) for a in (x, dy, log_rate, rotation)))


def inner_kernel(n, x_buf, dy_buf, lr_ref, ro_ref, rr_ref, ri_ref, *refs):
    out_ref, coef_ref, xp_ref, yp_ref, blk_ref, mid_ref, table_ref, head_ref, turn_ref, tx, ty, corr, state, acc = refs
    steps, width = x_buf.shape
    me = lax.axis_index("ctx")
    modes = lr_ref.shape[0]
    share = min(width, GROUP_W)
    groups = width // share
    blocks = steps // L
    base = first_group(width)
    offset = positions(modes)
    row = lax.broadcasted_iota(jnp.int32, (L, L), 0)
    lane = lax.broadcasted_iota(jnp.int32, (L, L), 1)
    out_lane = lax.broadcasted_iota(jnp.int32, (modes, LANES), 1)
    m2, m3, m4 = 2 * modes, 3 * modes, 4 * modes
    coeffs = []
    for g in range(groups):
        rate = jnp.exp(group_column(lr_ref, base + g))
        angle = group_column(ro_ref, base + g)
        real = group_column(rr_ref, base + g)
        imag = group_column(ri_ref, base + g)
        decay = jnp.exp(-2.0 * rate)
        gain = jnp.sqrt(complement(rate, decay))
        leap = powers(rate, angle, float(L))
        behind = (L - 1.0) - offset
        back = powers(rate, angle, behind)
        ahead = powers(rate, angle, offset)
        lags = jnp.sum(gain * (real * ahead[0] - imag * ahead[1]), axis=0, keepdims=True)
        ahead = conj(ahead)
        tx[g] = split([*back, *scale(behind, back)])
        later = conj(powers(rate, angle, jnp.maximum(offset - HALF, 0.0)))
        later = [jnp.where(offset >= HALF, part, 0.0) for part in later]
        ty[g, : 2 * m4, :] = split([*ahead, *scale(offset + 1.0, ahead)])
        ty[g, 2 * m4 :, :] = split(later)
        rows = jnp.broadcast_to(lags[:, :HALF], (HALF, HALF))
        bit = 1
        while bit < HALF:
            shifted = (row[:HALF, :HALF] & bit) != 0
            rows = jnp.where(shifted, pltpu.roll(rows, bit, 1), rows)
            bit *= 2
        upper = lane[:HALF, :HALF] >= row[:HALF, :HALF]
        table_ref[g, :, :HALF] = jnp.where(upper, rows, 0.0).astype(bf16)
        far = powers(rate, angle, float(HALF) - offset[:, :HALF])
        pulls = [gain * (real * far[0] - imag * far[1]), gain * (real * far[1] + imag * far[0])]
        pulls = pulls + pulls + [jnp.zeros((LANES - m4, HALF), f32)]
        table_ref[g, :, HALF:] = jnp.concatenate(pulls, axis=0).T[:, :m4].astype(bf16)
        half = powers(rate, angle, float(HALF))
        step = powers(rate, angle, 1.0)
        coeffs.append((rate, angle, leap, ahead, step))
        whole = powers(rate, angle, float(steps))
        column = [real, imag, rate, gain, decay / gain, *step, *leap, *half]
        reaches = [(jnp.ones_like(rate), jnp.zeros_like(rate))]
        for s in range(2, n):
            reaches.append(cmul(reaches[-1], whole))
        for s in range(1, n):
            future = conj(reaches[n - s - 1])
            for part in range(2):
                factor = jnp.where(me - s >= 0, reaches[s - 1][part], future[part])
                turn_ref[g, s - 1, part] = jnp.broadcast_to(factor, (modes, LANES))
        table = jnp.zeros((modes, LANES), f32)
        for k, value in enumerate(column):
            table = jnp.where(out_lane == k, value, table)
        coef_ref[g] = table
    state[...] = jnp.zeros_like(state)
    acc[...] = jnp.zeros_like(acc)
    yp_ref[...] = jnp.zeros_like(yp_ref)
    corr[...] = jnp.zeros_like(corr)
    reach = [(jnp.ones_like(coeffs[0][0]), jnp.zeros_like(coeffs[0][0]))] * groups
    for b in range(blocks):
        rows = slice(b * L, (b + 1) * L)
        for g in range(groups):
            leap = coeffs[g][2]
            cols = slice(g * share, (g + 1) * share)
            xb = x_buf[rows, cols]
            yb = dy_buf[rows, cols]
            corr[g] += lax.dot_general(xb, yb, (((1,), (1,)), ((), ())), preferred_element_type=f32)
            xs = dot(tx[g], xb)
            xs = xs[:m4] + xs[m4:]
            ys = dot(ty[g], yb)
            mid = ys[2 * m4 : 2 * m4 + m2] + ys[2 * m4 + m2 :]
            mid_ref[b * m2 : (b + 1) * m2, cols] = mid.astype(bf16)
            ys = ys[:m4] + ys[m4 : 2 * m4]
            blk_ref[b * m2 : (b + 1) * m2, cols] = ys[:m2].astype(bf16)
            x0, x1 = (xs[:modes], xs[modes:m2]), (xs[m2:m3], xs[m3:])
            y0, y1 = (ys[:modes], ys[modes:m2]), (ys[m2:m3], ys[m3:])
            e = state[0:modes, cols], state[modes:m2, cols]
            ep = state[m2:m3, cols], state[m3:m4, cols]
            third = cdot(e, y0)
            second = add(cdot(ep, y0), cdot(e, y1))
            acc[0:modes, cols] += third[0]
            acc[modes:m2, cols] += third[1]
            acc[m2:m3, cols] += second[0]
            acc[m3:m4, cols] += second[1]
            ep = add(cmul(leap, add(ep, scale(float(L), e))), x1)
            e = add(cmul(leap, e), x0)
            state[0:modes, cols], state[modes:m2, cols] = e
            state[m2:m3, cols], state[m3:m4, cols] = ep
            far = add(y1, scale(float(b * L), y0))
            far = cmul(conj(reach[g]), far)
            yp_ref[0:modes, cols] += far[0]
            yp_ref[modes:m2, cols] += far[1]
            reach[g] = cmul(reach[g], leap)
    xp_ref[...] = state[m2:m4, :]
    head_ref[...] = dy_buf[: HEAD * HALF, :].reshape(head_ref.shape)
    out = jnp.zeros((modes, LANES), f32)
    for g in range(groups):
        rate, angle, leap, ahead, step = coeffs[g]
        cols = slice(g * share, (g + 1) * share)
        lagged = jnp.where(lane >= row, corr[g], 0.0)
        bit = 1
        while bit < L:
            lagged = jnp.where((row & bit) != 0, pltpu.roll(lagged, L - bit, 1), lagged)
            bit *= 2
        lags = jnp.sum(lagged, axis=0, keepdims=True)
        third = cmul(conj(step), (lane_sum(acc[0:modes, cols]), lane_sum(acc[modes:m2, cols])))
        second = lane_sum(acc[m2:m3, cols]), lane_sum(acc[m3:m4, cols])
        third = add(third, (lane_sum(ahead[0] * lags), lane_sum(ahead[1] * lags)))
        prior = conj(powers(rate, angle, jnp.maximum(offset - 1.0, 0.0)))
        ramp = offset * lags
        second = add(second, (lane_sum(prior[0] * ramp), lane_sum(prior[1] * ramp)))
        for q, value in enumerate((*third, *second)):
            out = jnp.where(out_lane == g * 4 + q, value, out)
    out_ref[...] = out


def complement(rate, decay):
    z = 2.0 * rate
    series = jnp.ones_like(z)
    for k in range(8, 1, -1):
        series = 1.0 - z / k * series
    return jnp.where(z < 0.5, z * series, 1.0 - decay)


def inner_sums(n, x, dy, params):
    steps, width = x.shape
    modes = params[0].shape[0]
    groups = max(1, width // GROUP_W)
    state = jax.ShapeDtypeStruct((2 * modes, width), f32)
    vmem = pl.BlockSpec(memory_space=pltpu.VMEM)
    return pl.pallas_call(
        functools.partial(inner_kernel, n),
        in_specs=[vmem] * 6,
        out_specs=[vmem] * 9,
        out_shape=[
            jax.ShapeDtypeStruct((modes, LANES), f32),
            jax.ShapeDtypeStruct((groups, modes, LANES), f32),
            state,
            state,
            jax.ShapeDtypeStruct((steps // L * 2 * modes, width), bf16),
            jax.ShapeDtypeStruct((steps // L * 2 * modes, width), bf16),
            jax.ShapeDtypeStruct((groups, HALF, HALF + 4 * modes), bf16),
            jax.ShapeDtypeStruct((HEAD, HALF, width), bf16),
            jax.ShapeDtypeStruct((groups, n - 1, 2, modes, LANES), f32),
        ],
        scratch_shapes=[
            pltpu.VMEM((groups, 8 * modes, L), bf16),
            pltpu.VMEM((groups, 12 * modes, L), bf16),
            pltpu.VMEM((groups, L, L), f32),
            pltpu.VMEM((4 * modes, width), f32),
            pltpu.VMEM((4 * modes, width), f32),
        ],
        cost_estimate=pl.CostEstimate(
            flops=8 * L * steps * width, bytes_accessed=4 * steps * width, transcendentals=0
        ),
        compiler_params=pltpu.CompilerParams(vmem_limit_bytes=SCOPED),
        name="inner_sums",
    )(*(pltpu.with_memory_space_constraint(a, pltpu.VMEM) for a in (x, dy)), *params)


def cross_kernel(n, steps, in_ref, coef_ref, turn_ref, e_ref, xp_ref, yp_ref, skip_ref, *refs):
    received = refs[: n - 1]
    send_ref, exit_ref, total_ref = refs[n - 1 :]
    modes = in_ref.shape[0]
    width = e_ref.shape[1]
    share = min(width, GROUP_W)
    groups = width // share
    tiles = width // LANES
    m2 = 2 * modes
    me = lax.axis_index("ctx")
    direct = skip_ref[...]
    for r in received:
        direct = direct + r[tiles * m2 :, :]
    total_ref[...] = direct
    own = in_ref[...]
    row = lax.broadcasted_iota(jnp.int32, (modes, send_ref.shape[1]), 0)
    lane = lax.broadcasted_iota(jnp.int32, (modes, send_ref.shape[1]), 1)
    out = jnp.zeros(row.shape, f32)
    for g in range(groups):
        real, imag, rate, gain, slope = (coef_ref[g, :, k : k + 1] for k in range(5))
        step = coef_ref[g, :, 5:6], coef_ref[g, :, 6:7]
        third = [jnp.zeros((modes, LANES), f32)] * 2
        second = [jnp.zeros((modes, LANES), f32)] * 2
        for t in range(g * share // LANES, (g + 1) * share // LANES):
            cols = slice(t * LANES, (t + 1) * LANES)
            zero = jnp.zeros((modes, LANES), f32)
            entry, exit_, drift = (zero, zero), (zero, zero), (zero, zero)
            for s in range(1, n):
                got = received[s - 1]
                value = got[t * m2 : t * m2 + modes, :], got[t * m2 + modes : (t + 1) * m2, :]
                term = cmul((turn_ref[g, s - 1, 0], turn_ref[g, s - 1, 1]), value)
                earlier = me - s >= 0
                entry = add(entry, [jnp.where(earlier, v, 0.0) for v in term])
                term = [jnp.where(earlier, 0.0, v) for v in term]
                exit_ = add(exit_, term)
                if s < n - 1:
                    drift = add(drift, scale(float(steps * (n - s - 1)), term))
            exit_ref[0:modes, cols] = exit_[0]
            exit_ref[modes:m2, cols] = exit_[1]
            e = e_ref[0:modes, cols], e_ref[modes:m2, cols]
            xp = xp_ref[0:modes, cols], xp_ref[modes:m2, cols]
            yp = yp_ref[0:modes, cols], yp_ref[modes:m2, cols]
            third = add(third, cdot(e, exit_))
            second = add(second, add(add(cdot(xp, exit_), cdot(e, drift)), cdot(entry, yp)))
        third = cmul(conj(step), (lane_sum(third[0]), lane_sum(third[1])))
        third = add(third, (own[:, g * 4 : g * 4 + 1], own[:, g * 4 + 1 : g * 4 + 2]))
        second = lane_sum(second[0]), lane_sum(second[1])
        second = add(second, (own[:, g * 4 + 2 : g * 4 + 3], own[:, g * 4 + 3 : g * 4 + 4]))
        first = scale(gain, third)
        second = scale(gain, second)
        twist = cdot((real, imag), second)
        gain_term = real * third[0] + imag * third[1]
        pulled = cdot(twist, step)
        grads = (rate * (slope * gain_term - pulled[0]), -pulled[1], first[0], first[1])
        for q, value in enumerate(grads):
            out = jnp.where(lane == (g * 4 + q) * modes + row, value, out)
    line = jnp.sum(out, axis=0, keepdims=True)
    send_ref[...] = jnp.broadcast_to(line, send_ref.shape)


def cross_terms(n, devices, steps, own, coef, turn, e, xp, yp, skip, received):
    groups, modes = coef.shape[:2]
    line = -(-groups * 4 * modes // LANES) * LANES
    vmem = pl.BlockSpec(memory_space=pltpu.VMEM)
    return pl.pallas_call(
        functools.partial(cross_kernel, n, steps),
        in_specs=[vmem] * (7 + n - 1),
        out_specs=[vmem] * 3,
        out_shape=[
            jax.ShapeDtypeStruct((devices, line), f32),
            jax.ShapeDtypeStruct(e.shape, f32),
            jax.ShapeDtypeStruct(skip.shape, f32),
        ],
        compiler_params=pltpu.CompilerParams(vmem_limit_bytes=SCOPED),
        name="cross_terms",
    )(own, coef, turn, e, xp, yp, skip, *received)


def input_kernel(dy_hbm, head_ref, table_ref, blk_ref, mid_ref, exit_ref, coef_ref, skip_ref, *refs):
    out_hbm, both, out_buf, sem = refs
    blocks, _, width = dy_hbm.shape
    modes = exit_ref.shape[0] // 2
    share = min(width, GROUP_W)
    groups = width // share
    m2 = 2 * modes
    cuts = last_cuts(blocks)
    copies = []
    for c, (start, count) in enumerate(cuts):
        part = pl.ds(start, count)
        copy = None
        if c > 0:
            copy = pltpu.make_async_copy(dy_hbm.at[part], both.at[part, pl.ds(0, HALF)], sem.at[0, c])
            copy.start()
        copies.append(copy)
    both[:HEAD, :HALF, :] = head_ref[...]
    for g in range(groups):
        cols = slice(g * share, (g + 1) * share)
        leap = coef_ref[g, :, 7:8], -coef_ref[g, :, 8:9]
        half = coef_ref[g, :, 9:10], -coef_ref[g, :, 10:11]
        a = exit_ref[0:modes, cols], exit_ref[modes:m2, cols]
        for b in reversed(range(blocks // 2)):
            rows = slice(b * m2, (b + 1) * m2)
            both[2 * b + 1, HALF:, cols] = split(a)
            mid = mid_ref[rows, cols].astype(f32)
            both[2 * b, HALF:, cols] = split(add(cmul(half, a), (mid[:modes], mid[modes:])))
            own = blk_ref[rows, cols].astype(f32)
            a = add(cmul(leap, a), (own[:modes], own[modes:]))
    outs = []
    for c, (start, count) in enumerate(cuts):
        if c > 0:
            copies[c].wait()
        for b in range(start, start + count):
            for g in range(groups):
                cols = slice(g * share, (g + 1) * share)
                direct = skip_ref[:, cols] * both[b, :HALF, cols].astype(f32)
                out_buf[b, :, cols] = (dot(table_ref[g], both[b, :, cols]) + direct).astype(bf16)
        part = pl.ds(start, count)
        outs.append(pltpu.make_async_copy(out_buf.at[part], out_hbm.at[part], sem.at[1, c]))
        outs[c].start()
    for copy in outs:
        copy.wait()


def last_cuts(blocks):
    per = CHUNK // HALF
    starts = [0, *range(HEAD, blocks, per), blocks - per // 2, blocks]
    return [(a, b - a) for a, b in zip(starts, starts[1:])]


def input_grad(dy, head, table, blk, mid, exit_state, coef, skip_gain):
    steps, width = dy.shape
    depth = table.shape[2]
    blocks = steps // HALF
    vmem = pl.BlockSpec(memory_space=pltpu.VMEM)
    hbm = pl.BlockSpec(memory_space=pltpu.HBM)
    dy = pltpu.with_memory_space_constraint(dy.reshape(blocks, HALF, width), pltpu.HBM)
    out = pl.pallas_call(
        input_kernel,
        in_specs=[hbm] + [vmem] * 7,
        out_specs=hbm,
        out_shape=jax.ShapeDtypeStruct((blocks, HALF, width), bf16),
        scratch_shapes=[
            pltpu.VMEM((blocks, depth, width), bf16),
            pltpu.VMEM((blocks, HALF, width), bf16),
            pltpu.SemaphoreType.DMA((2, len(last_cuts(blocks)))),
        ],
        cost_estimate=pl.CostEstimate(
            flops=4 * HALF * steps * width, bytes_accessed=4 * steps * width, transcendentals=0
        ),
        compiler_params=pltpu.CompilerParams(vmem_limit_bytes=SCOPED),
        name="input_grad",
    )(dy, head, table, blk, mid, exit_state, coef, skip_gain)
    return out.reshape(steps, width)


def total_kernel(parts, width, in_ref, *outs):
    devices, line = in_ref.shape
    columns = devices // parts
    modes, groups = outs[0].shape
    local_groups = max(1, width // GROUP_W)
    table = in_ref[...]
    total = table[0:columns]
    for p in range(1, parts):
        total = total + table[p * columns : (p + 1) * columns]
    pad = -(-columns // LANES) * LANES - columns
    if pad:
        total = jnp.concatenate([total, jnp.zeros((pad, line), f32)], axis=0)
    turned = total.T
    group = lax.broadcasted_iota(jnp.int32, (modes, groups), 1)
    for q in range(4):
        result = jnp.zeros((modes, groups), f32)
        for c in range(columns):
            for g in range(local_groups):
                start = (g * 4 + q) * modes
                value = turned[start : start + modes, c : c + 1]
                place = group == c * width // GROUP_W + g
                result = result + jnp.where(place, value, 0.0)
        outs[q][...] = result


def totals(parts, width, shape, gathered):
    vmem = pl.BlockSpec(memory_space=pltpu.VMEM)
    return pl.pallas_call(
        functools.partial(total_kernel, parts, width),
        in_specs=[vmem],
        out_specs=[vmem] * 4,
        out_shape=[jax.ShapeDtypeStruct(shape, f32)] * 4,
        compiler_params=pltpu.CompilerParams(vmem_limit_bytes=SCOPED),
        name="totals",
    )(gathered)


def local(x, dy, log_rate, rotation, res_re, res_im, skip_gain):
    steps, width = x.shape
    n = lax.axis_size("ctx")
    devices = n * lax.axis_size("ch")
    params = (log_rate, rotation, res_re, res_im)
    *sends, e, skip, x_near, dy_near = shard_sums(n, x, dy, log_rate, rotation)
    received = [
        lax.ppermute(part, "ctx", [(i, (i + s) % n) for i in range(n)])
        for s, part in enumerate(sends, 1)
    ]
    own, coef, xp, yp, blk, mid, table, head, turn = inner_sums(n, x_near, dy_near, params)
    line, exit_state, direct = cross_terms(n, devices, steps, own, coef, turn, e, xp, yp, skip, received)
    gathered = lax.all_to_all(line, ("ctx", "ch"), 0, 0, tiled=True)
    grad_input = input_grad(
        dy, head, table, blk, mid, exit_state, coef, skip_gain.reshape(1, width)
    )
    grads = totals(n, width, log_rate.shape, gathered)
    return (grad_input, *grads, direct[: width // LANES].reshape(width))


def solution(mesh):
    placed = (P("ctx", "ch"), P("ctx", "ch"), P(), P(), P(), P(), P("ch"))
    return jax.shard_map(
        local,
        mesh=mesh,
        in_specs=placed,
        out_specs=(P("ctx", "ch"), P(), P(), P(), P(), P("ch")),
        check_vma=False,
    )
```
